512 devices in a mesh: field: 32 (over z_hi, x, core), point: 16 (over y, z_lo).
Axes of the slice: x: 4, y: 4, z: 16 (z_hi: 4, z_lo: 4; z = z_hi * 4 + z_lo), core: 2. Of those that a mesh axis runs over, the one named last changes fastest.
Arguments:
- residual_in: bfloat16 [32, 4096, 2048], P('field', 'point'), may hold values from -6 to 6
- coefs_in: bfloat16 [32, 4096, 4, 256], P('field', 'point'), may hold values from 0 to 1
- dictionary: bfloat16 [8192, 2048], P('field'), may hold values from -0.125 to 0.125
- owner_order: int32 [32], replicated, may hold values from 0 to 31, each once
- pixel_of: int32 [32, 4096], P('field', 'point'), may hold values from 0 to 4095, each once within a row
Outputs:
- maps: float32 [32, 4, 256, 32, 128], P('field', None, 'point')
The draws below stay inside these ranges and needn't reach their ends.
Inputs may be any that keep to these rules, and one draw needn't show every extreme that they name: `owner_order`: A permutation of the dictionary blocks. `pixel_of`: each field's row is a permutation of its scan points over the 32 x 128 pixels.
All inputs are finite; a program needn't handle non-finite values.
Results may differ from the reference program's by a relative error of at most 0.00045.
Values may be sent and summed in bfloat16 or wider, within the bound.
A program may use at most 64 MiB of HBM per device.

```python
import jax
import jax.numpy as jnp
from jax import lax

F = 2048
KB = 256
TURNS = 4
SWEEPS = 4
MAP_W = 128
NPTS = 4096
TEMPLATES = 8192
N_FIELD = 32


def shard_levels(stream_key, shape, cuts, smallest, high):
    def one(position, parts):
        heights = jax.random.uniform(jax.random.fold_in(jax.random.fold_in(stream_key, 6), position), (parts,), jnp.float32, smallest / len(cuts), high / len(cuts))
        return jnp.repeat(jnp.exp(heights), shape[position] // parts).reshape((-1,) + (1,) * (len(shape) - position - 1))

    gain = one(*cuts[0])
    for cut in cuts[1:]:
        gain = gain * one(*cut)
    return gain


def bell_draw(stream_key, shape, deviation, bound, pieces=(), dtype=jnp.bfloat16):
    entries = deviation * jax.random.normal(stream_key, shape, jnp.float32)
    if pieces:
        entries = entries * shard_levels(stream_key, shape, pieces, -0.22, 0.18)
    return jnp.clip(entries, -bound, bound).astype(dtype)


def setup_inputs(seed: int = 0) -> dict:
    splits = jax.random.split(jax.random.key(seed), 6)
    residual_in = bell_draw(splits[0], (N_FIELD, NPTS, F), 1.0, 6.0, ((0, 32), (1, 16)))
    coefs_in = jnp.clip(1.0 * jax.random.uniform(splits[1], (N_FIELD, NPTS, TURNS, KB), jnp.float32) ** shard_levels(splits[1], (N_FIELD, NPTS, TURNS, KB), ((0, 32), (1, 16)), -0.2, 0.2), 0.0, 1.0).astype(jnp.bfloat16)
    dictionary = bell_draw(splits[2], (TEMPLATES, F), F ** -0.5, 0.125, ((0, 32),))
    owner_order = jax.random.permutation(splits[3], N_FIELD).astype(jnp.int32)
    pixel_of = jax.vmap(lambda own: jax.random.permutation(own, NPTS))(jax.random.split(splits[4], N_FIELD)).reshape((N_FIELD, NPTS)).astype(jnp.int32)
    return {"residual_in": residual_in, "coefs_in": coefs_in, "dictionary": dictionary, "owner_order": owner_order, "pixel_of": pixel_of}


time_step = 0.2
edge_scale = 0.5


def block_steps(templates):
    gram = lax.dot_general(templates, templates, (((1,), (1,)), ((), ())), preferred_element_type=jnp.float32)
    return 1.0 / jnp.sum(jnp.abs(gram), axis=1)


def diffuse(grids):
    for repeat in range(SWEEPS):
        padded = jnp.pad(grids, ((0, 0), (1, 1), (1, 1)), mode="edge")
        summed = jnp.zeros_like(grids)
        for neighbour in (padded[:, :-2, 1:-1], padded[:, 2:, 1:-1], padded[:, 1:-1, :-2], padded[:, 1:-1, 2:]):
            differ = neighbour - grids
            scaled = differ / edge_scale
            summed = summed + differ / (1.0 + scaled * scaled)
        grids = grids + time_step * summed
    return grids


def reference(residual_in, coefs_in, dictionary, owner_order, pixel_of):
    blocks = dictionary.reshape(N_FIELD, KB, F)
    chosen = []
    steps_all = []
    for turn_index in range(TURNS):
        templates = blocks[owner_order[turn_index]]
        chosen.append(templates)
        steps_all.append(block_steps(templates))

    def one_field(inputs):
        residual, coefs, pixel_ids = inputs
        coefs = coefs.astype(jnp.float32)
        updated = []
        for turn_index in range(TURNS):
            templates = chosen[turn_index]
            correlation = lax.dot_general(residual, templates, (((1,), (1,)), ((), ())), preferred_element_type=jnp.float32)
            before = coefs[:, turn_index, :]
            after = jnp.maximum(before + steps_all[turn_index][None, :] * correlation, 0.0)
            updated.append(after)
            if turn_index + 1 < TURNS:
                change = (after - before).astype(jnp.bfloat16)
                residual = (residual.astype(jnp.float32) - jnp.dot(change, templates, preferred_element_type=jnp.float32)).astype(jnp.bfloat16)
        stacked = jnp.stack(updated, axis=1)
        values = stacked.reshape(NPTS, TURNS * KB).T
        flat = jnp.zeros((TURNS * KB, NPTS), jnp.float32).at[:, pixel_ids].set(values)
        grids = diffuse(flat.reshape(TURNS * KB, NPTS // MAP_W, MAP_W))
        return grids.reshape(TURNS, KB, NPTS // MAP_W, MAP_W)

    return lax.map(one_field, (residual_in, coefs_in, pixel_of))
```

```python
import functools

import jax
import jax.numpy as jnp
from jax import lax
from jax.experimental import pallas as pl
from jax.experimental.pallas import tpu as pltpu
from jax.sharding import PartitionSpec as P

TURNS = 4
SWEEPS = 4
MAP_W = 128
MESH = pl.DeviceIdType.MESH

time_step = 0.2
edge_scale = 0.5


def dev(z, x, core, y):
    return (z // 4 * 8 + x * 2 + core, y * 4 + z % 4)


def remote(src, dst, send, recv, device):
    return pltpu.make_async_remote_copy(
        src_ref=src, dst_ref=dst, send_sem=send, recv_sem=recv, device_id=device, device_id_type=MESH
    )


def gather_kernel(
    owner, block, g, cand, a_send, a_recv, b_send, b_recv, own_sem, z_send, z_recv, ring_send, ring_recv, c_send, c_recv
):
    f = lax.axis_index("field")
    p = lax.axis_index("point")
    core = f % 2
    chip = f // 2
    x = chip % 4
    zh = f // 8
    y = p // 4
    z = zh * 4 + p % 4
    sibling = (f + 1 - 2 * core, p)

    barrier = pltpu.get_barrier_semaphore()

    def greet(device):
        pl.semaphore_signal(barrier, inc=1, device_id=device, device_id_type=MESH)

    def greet_field(i, _):
        greet(((chip + i) % 16 * 2 + core, p))
        return _

    lax.fori_loop(1, 16, greet_field, 0)

    def greet_z(i, _):
        @pl.when(i % 4 != 0)
        def _greet():
            greet(dev((z + i) % 16, x, core, y))

        return _

    lax.fori_loop(1, 16, greet_z, 0)
    for step in (1, 3):
        greet(dev(z, x, core, (y + step) % 4))
    greet(sibling)
    pl.semaphore_wait(barrier, 15 + 12 + 2 + 1)

    lanes = pl.ds(pl.multiple_of(p * 128, 128), 128)

    def tile_of(to):
        return block.at[pl.ds(pl.multiple_of(to * 16, 16), 16), lanes]

    def scatter(i, _):
        to = (chip + i) % 16
        remote(tile_of(to), cand.at[core, chip], a_send, a_recv, (to * 2 + core, p)).start()
        return _

    lax.fori_loop(1, 16, scatter, 0)
    own = pltpu.make_async_copy(tile_of(chip), cand.at[core, chip], own_sem)
    own.start()
    own.wait()
    all_a = remote(cand.at[0, pl.ds(0, 15)], cand.at[0, pl.ds(0, 15)], a_send, a_recv, sibling)
    all_a.wait_recv()
    both = remote(cand.at[core], cand.at[core], b_send, b_recv, sibling)
    both.start()
    all_a.wait_send()
    both.wait()

    mine = pl.ds(pl.multiple_of(x * 16, 16), 16)
    for tt in range(2):
        o = owner[core + 2 * tt]
        g[core, tt, p, zh, mine, :] = cand[o % 2, o // 2]

    def along_z(i, _):
        part = g.at[core, :, p, zh, mine, :]
        remote(part, part, z_send, z_recv, dev((z + i) % 16, x, core, y)).start()
        return _

    lax.fori_loop(1, 16, along_z, 0)
    amount = g.at[0, 0, pl.ds(0, 15), 0, pl.ds(0, 32), :]
    all_z = remote(amount, amount, z_send, z_recv, sibling)
    all_z.wait_recv()
    all_z.wait_send()

    def ring(stage, neighbour, region):
        def make(t, kind):
            offset, half, to = ((0, None, 1), (0, None, 3), (3, 0, 1), (1, 1, 3))[kind]
            ref = g.at[region(t, offset, half)]
            return remote(ref, ref, ring_send.at[stage, kind, t], ring_recv.at[stage, kind, t], neighbour(to))

        def start(t):
            make(t, 0).start()
            make(t, 1).start()

        def forward(t):
            make(t, 0).wait_recv()
            make(t, 2).start()
            make(t, 1).wait_recv()
            make(t, 3).start()

        def finish(t):
            make(t, 2).wait_recv()
            make(t, 3).wait_recv()

        def drain(t):
            for kind in range(4):
                make(t, kind).wait_send()

        return start, forward, finish, drain

    def along(axis):
        def neighbour(step):
            if axis == "x":
                return dev(z, (x + step) % 4, core, y)
            return dev(z, x, core, (y + step) % 4)

        return neighbour

    def mid_region(axis):
        def region(t, offset, half):
            bx = (x + offset) % 4 if axis == "x" else x
            by = (y + offset) % 4 if axis == "y" else y
            points = pl.ds(by * 4, 4) if half is None else pl.ds(by * 4 + 2 * half, 2)
            return (core, t // 2, points, pl.ds(t % 2 * 2, 2), pl.ds(pl.multiple_of(bx * 16, 16), 16), slice(None))

        return region

    def last_region(axis):
        def region(t, offset, half):
            if axis == "x":
                points = pl.ds(0, 16) if half is None else pl.ds(8 * half, 8)
                rows = pl.ds(pl.multiple_of((x + offset) % 4 * 16, 16), 16)
            else:
                by = (y + offset) % 4
                points = pl.ds(by * 4, 4) if half is None else pl.ds(by * 4 + 2 * half, 2)
                rows = slice(None)
            return (core, t // 2, points, pl.ds(t % 2 * 2, 2), rows, slice(None))

        return region

    def swap(t):
        part = g.at[core, t // 2, :, pl.ds(t % 2 * 2, 2)]
        return remote(part, part, c_send.at[t], c_recv.at[t], sibling)

    def rings(first, last):
        m_start, m_forward, m_finish, m_drain = ring(0, along(first), mid_region(first))
        l_start, l_forward, l_finish, l_drain = ring(1, along(last), last_region(last))
        for t in range(TURNS):
            m_start(t)
        for t in range(TURNS):
            m_forward(t)
            m_finish(t)
            l_start(t)
        for t in range(TURNS):
            l_forward(t)
            l_finish(t)
            swap(t).start()
        for t in range(TURNS):
            m_drain(t)
            l_drain(t)

    @pl.when(core == 0)
    def _even():
        rings("y", "x")

    @pl.when(core == 1)
    def _odd():
        rings("x", "y")

    for t in range(TURNS):
        swap(t).wait()


def gather_blocks(owner_order, dictionary):
    return pl.pallas_call(
        gather_kernel,
        name="gather_blocks",
        out_shape=jax.ShapeDtypeStruct((2, 2, 16, 4, 64, 128), jnp.bfloat16),
        in_specs=[pl.BlockSpec(memory_space=pltpu.SMEM), pl.BlockSpec(memory_space=pl.ANY)],
        out_specs=pl.BlockSpec(memory_space=pltpu.VMEM),
        scratch_shapes=[
            pltpu.VMEM((2, 16, 16, 128), jnp.bfloat16),
            pltpu.SemaphoreType.DMA,
            pltpu.SemaphoreType.DMA,
            pltpu.SemaphoreType.DMA,
            pltpu.SemaphoreType.DMA,
            pltpu.SemaphoreType.DMA,
            pltpu.SemaphoreType.DMA,
            pltpu.SemaphoreType.DMA,
            pltpu.SemaphoreType.DMA((2, 4, TURNS)),
            pltpu.SemaphoreType.DMA((2, 4, TURNS)),
            pltpu.SemaphoreType.DMA((TURNS,)),
            pltpu.SemaphoreType.DMA((TURNS,)),
        ],
        compiler_params=pltpu.CompilerParams(collective_id=0, has_side_effects=True, vmem_limit_bytes=16 << 20),
    )(owner_order, dictionary)


def block_steps(templates):
    gram = lax.dot_general(
        templates, templates, (((1,), (1,)), ((), ())), preferred_element_type=jnp.float32
    )
    return 1.0 / jnp.sum(jnp.abs(gram), axis=1)


def diffuse(grids):
    for repeat in range(SWEEPS):
        padded = jnp.pad(grids, ((0, 0), (1, 1), (1, 1)), mode="edge")
        summed = jnp.zeros_like(grids)
        for neighbour in (
            padded[:, :-2, 1:-1],
            padded[:, 2:, 1:-1],
            padded[:, 1:-1, :-2],
            padded[:, 1:-1, 2:],
        ):
            differ = neighbour - grids
            scaled = differ / edge_scale
            summed = summed + differ / (1.0 + scaled * scaled)
        grids = grids + time_step * summed
    return grids


def build_maps(moved, pixel_ids):
    points = moved.shape[0]
    count = moved.shape[1]
    local_kb = moved.shape[2]
    values = moved.reshape(points, count * local_kb).T
    flat = jnp.zeros((count * local_kb, points), jnp.float32).at[:, pixel_ids].set(values)
    grids = diffuse(flat.reshape(count * local_kb, points // MAP_W, MAP_W))
    return grids.reshape(count, local_kb, points // MAP_W, MAP_W)


def per_device(residual_in, coefs_in, dictionary, owner_order, pixel_of):
    residual = residual_in[0]
    coefs = coefs_in[0].astype(jnp.float32)
    pixel_ids = lax.all_gather(pixel_of[0], "point", axis=0, tiled=True)
    updated = []
    gathered = gather_blocks(owner_order, dictionary)
    for turn_index in range(TURNS):
        templates = gathered[turn_index % 2, turn_index // 2].transpose(1, 2, 0, 3).reshape(256, 2048)
        step_size = block_steps(templates)
        correlation = lax.dot_general(
            residual, templates, (((1,), (1,)), ((), ())), preferred_element_type=jnp.float32
        )
        before = coefs[:, turn_index, :]
        after = jnp.maximum(before + step_size[None, :] * correlation, 0.0)
        updated.append(after)
        if turn_index + 1 < TURNS:
            change = (after - before).astype(jnp.bfloat16)
            residual = (
                residual.astype(jnp.float32)
                - jnp.dot(change, templates, preferred_element_type=jnp.float32)
            ).astype(jnp.bfloat16)
    stacked = jnp.stack(updated, axis=1)
    maps = build_maps(
        lax.all_to_all(stacked, "point", split_axis=2, concat_axis=0, tiled=True), pixel_ids
    )
    return maps[None]


def solution(mesh):
    placed = (
        P("field", "point", None),
        P("field", "point", None, None),
        P("field", None),
        P(),
        P("field", "point"),
    )
    return jax.shard_map(
        per_device,
        mesh=mesh,
        in_specs=placed,
        out_specs=P("field", None, "point", None, None),
        check_vma=False,
    )
```

```python
import functools

import jax
import jax.numpy as jnp
from jax import lax
from jax.experimental import pallas as pl
from jax.experimental.pallas import tpu as pltpu
from jax.sharding import PartitionSpec as P

TURNS = 4
SWEEPS = 4
MAP_W = 128
MESH = pl.DeviceIdType.MESH

time_step = 0.2
edge_scale = 0.5


def dev(z, x, core, y):
    return (z // 4 * 8 + x * 2 + core, y * 4 + z % 4)


def remote(src, dst, send, recv, device):
    return pltpu.make_async_remote_copy(
        src_ref=src, dst_ref=dst, send_sem=send, recv_sem=recv, device_id=device, device_id_type=MESH
    )


def nt(a, b):
    return lax.dot_general(a, b, (((1,), (1,)), ((), ())), preferred_element_type=jnp.float32)


def unmix_kernel(
    owner,
    block,
    residual_hbm,
    coefs,
    pixel_of,
    values,
    pixels,
    g,
    cand,
    residual,
    templates,
    updated,
    a_send,
    a_recv,
    b_send,
    b_recv,
    own_sem,
    z_send,
    z_recv,
    ring_send,
    ring_recv,
    c_send,
    c_recv,
    id_send,
    id_recv,
    v_send,
    v_recv,
    r_sem,
):
    f = lax.axis_index("field")
    p = lax.axis_index("point")
    core = f % 2
    chip = f // 2
    x = chip % 4
    zh = f // 8
    y = p // 4
    z = zh * 4 + p % 4
    sibling = (f + 1 - 2 * core, p)

    fetch = pltpu.make_async_copy(residual_hbm, residual, r_sem)
    fetch.start()
    barrier = pltpu.get_barrier_semaphore()

    def greet(device):
        pl.semaphore_signal(barrier, inc=1, device_id=device, device_id_type=MESH)

    def greet_field(i, _):
        greet(((chip + i) % 16 * 2 + core, p))
        return _

    lax.fori_loop(1, 16, greet_field, 0)

    def greet_z(i, _):
        @pl.when(i % 4 != 0)
        def _greet():
            greet(dev((z + i) % 16, x, core, y))

        return _

    lax.fori_loop(1, 16, greet_z, 0)

    def greet_point(i, _):
        to = (p + i) % 16

        @pl.when(to // 4 != y)
        def _greet():
            greet((f, to))

        return _

    lax.fori_loop(1, 16, greet_point, 0)
    greet(sibling)
    pl.semaphore_wait(barrier, 15 + 12 + 12 + 1)

    lanes = pl.ds(pl.multiple_of(p * 128, 128), 128)

    def tile_of(to):
        return block.at[pl.ds(pl.multiple_of(to * 16, 16), 16), lanes]

    def scatter(i, _):
        to = (chip + i) % 16
        remote(tile_of(to), cand.at[core, chip], a_send, a_recv, (to * 2 + core, p)).start()
        return _

    lax.fori_loop(1, 16, scatter, 0)

    def tell_pixels(i, _):
        remote(pixel_of, pixels.at[p], id_send, id_recv, (f, (p + i) % 16)).start()
        return _

    lax.fori_loop(1, 16, tell_pixels, 0)
    pixels[p] = pixel_of[...]
    own = pltpu.make_async_copy(tile_of(chip), cand.at[core, chip], own_sem)
    own.start()
    own.wait()
    all_a = remote(cand.at[0, pl.ds(0, 15)], cand.at[0, pl.ds(0, 15)], a_send, a_recv, sibling)
    all_a.wait_recv()
    both = remote(cand.at[core], cand.at[core], b_send, b_recv, sibling)
    both.start()
    all_a.wait_send()
    both.wait()

    mine = pl.ds(pl.multiple_of(x * 16, 16), 16)
    for tt in range(2):
        o = owner[core + 2 * tt]
        g[core, tt, p, zh, mine, :] = cand[o % 2, o // 2]

    def along_z(i, _):
        part = g.at[core, :, p, zh, mine, :]
        remote(part, part, z_send, z_recv, dev((z + i) % 16, x, core, y)).start()
        return _

    lax.fori_loop(1, 16, along_z, 0)
    amount = g.at[0, 0, pl.ds(0, 15), 0, pl.ds(0, 32), :]
    all_z = remote(amount, amount, z_send, z_recv, sibling)
    all_z.wait_recv()
    all_z.wait_send()

    def ring(stage, neighbour, region):
        def make(t, kind):
            offset, half, to = ((0, None, 1), (0, None, 3), (3, 0, 1), (1, 1, 3))[kind]
            ref = g.at[region(t, offset, half)]
            return remote(ref, ref, ring_send.at[stage, kind, t], ring_recv.at[stage, kind, t], neighbour(to))

        def start(t):
            make(t, 0).start()
            make(t, 1).start()

        def forward(t):
            make(t, 0).wait_recv()
            make(t, 2).start()
            make(t, 1).wait_recv()
            make(t, 3).start()

        def finish(t):
            make(t, 2).wait_recv()
            make(t, 3).wait_recv()

        def drain(t):
            for kind in range(4):
                make(t, kind).wait_send()

        return start, forward, finish, drain

    def along(axis):
        def neighbour(step):
            if axis == "x":
                return dev(z, (x + step) % 4, core, y)
            return dev(z, x, core, (y + step) % 4)

        return neighbour

    def mid_region(axis):
        def region(t, offset, half):
            bx = (x + offset) % 4 if axis == "x" else x
            by = (y + offset) % 4 if axis == "y" else y
            points = pl.ds(by * 4, 4) if half is None else pl.ds(by * 4 + 2 * half, 2)
            return (core, t // 2, points, pl.ds(t % 2 * 2, 2), pl.ds(pl.multiple_of(bx * 16, 16), 16), slice(None))

        return region

    def last_region(axis):
        def region(t, offset, half):
            if axis == "x":
                points = pl.ds(0, 16) if half is None else pl.ds(8 * half, 8)
                rows = pl.ds(pl.multiple_of((x + offset) % 4 * 16, 16), 16)
            else:
                by = (y + offset) % 4
                points = pl.ds(by * 4, 4) if half is None else pl.ds(by * 4 + 2 * half, 2)
                rows = slice(None)
            return (core, t // 2, points, pl.ds(t % 2 * 2, 2), rows, slice(None))

        return region

    def swap(t):
        part = g.at[core, t // 2, :, pl.ds(t % 2 * 2, 2)]
        return remote(part, part, c_send.at[t], c_recv.at[t], sibling)

    def rings(first, last):
        return ring(0, along(first), mid_region(first)), ring(1, along(last), last_region(last))

    def by_core(act):
        @pl.when(core == 0)
        def _even():
            act(*rings("y", "x"))

        @pl.when(core == 1)
        def _odd():
            act(*rings("x", "y"))

    def open_rings(mid, last):
        for t in range(TURNS):
            mid[0](t)
        for t in range(TURNS):
            mid[1](t)
            mid[2](t)
            last[0](t)

    def first_half(mid, last):
        for t in (0, 1):
            last[1](t)
            last[2](t)
            swap(t).start()

    def middle(mid, last):
        last[1](2)

    def second_half(mid, last):
        last[1](3)
        for t in (2, 3):
            last[2](t)
            swap(t).start()

    def close(mid, last):
        for t in range(TURNS):
            mid[3](t)
            last[3](t)

    def send_rows(t, to):
        rows = pl.ds(pl.multiple_of(to * 16, 16), 16)
        points = pl.ds(pl.multiple_of(p * 256, 256), 256)
        return updated.at[t, rows], values.at[t, :, points]

    def turn(t):
        for q in range(16):
            templates[:, 128 * q : 128 * (q + 1)] = g[t % 2, t // 2, q].reshape(256, 128)
        gram = nt(templates[...], templates[...])
        step = 1.0 / jnp.sum(jnp.abs(gram), axis=1, keepdims=True)
        before = coefs[t].astype(jnp.float32)
        after = jnp.maximum(before + step * nt(templates[...], residual[...]), 0.0)
        updated[t] = after

        def deliver(i, _):
            to = (p + i) % 16
            src, dst = send_rows(t, to)
            remote(src, dst, v_send.at[t], v_recv.at[t], (f, to)).start()
            return _

        lax.fori_loop(1, 16, deliver, 0)
        rows = pl.ds(pl.multiple_of(p * 16, 16), 16)
        values[t, :, pl.ds(pl.multiple_of(p * 256, 256), 256)] = updated[t, rows, :]
        if t + 1 < TURNS:
            change = (after - before).astype(jnp.bfloat16)
            for q in range(4):
                cols = slice(512 * q, 512 * (q + 1))
                moved = lax.dot_general(
                    change, templates[:, cols], (((0,), (0,)), ((), ())), preferred_element_type=jnp.float32
                )
                residual[:, cols] = (residual[:, cols].astype(jnp.float32) - moved).astype(jnp.bfloat16)

    by_core(open_rings)
    fetch.wait()
    by_core(first_half)
    swap(0).wait_recv()
    swap(1).wait_recv()
    turn(0)
    by_core(middle)
    turn(1)
    by_core(second_half)
    swap(2).wait_recv()
    swap(3).wait_recv()
    turn(2)
    turn(3)
    by_core(close)
    for t in range(TURNS):
        swap(t).wait_send()
    ids = remote(pixels.at[pl.ds(0, 15)], pixels.at[pl.ds(0, 15)], id_send, id_recv, sibling)
    ids.wait_send()
    ids.wait_recv()
    for t in range(TURNS):
        amount = values.at[t, :, pl.ds(0, 15 * 256)]
        done = remote(amount, amount, v_send.at[t], v_recv.at[t], sibling)
        done.wait_send()
        done.wait_recv()


def unmix(owner_order, dictionary, residual, coefs, pixel_of):
    vmem = pl.BlockSpec(memory_space=pltpu.VMEM)
    hbm = pl.BlockSpec(memory_space=pl.ANY)
    dma = pltpu.SemaphoreType.DMA
    return pl.pallas_call(
        unmix_kernel,
        name="unmix",
        out_shape=(
            jax.ShapeDtypeStruct((TURNS, 16, 4096), jnp.float32),
            jax.ShapeDtypeStruct((16, 1, 256), jnp.int32),
        ),
        in_specs=[pl.BlockSpec(memory_space=pltpu.SMEM), hbm, hbm, vmem, vmem],
        out_specs=(vmem, vmem),
        scratch_shapes=[
            pltpu.VMEM((2, 2, 16, 4, 64, 128), jnp.bfloat16),
            pltpu.VMEM((2, 16, 16, 128), jnp.bfloat16),
            pltpu.VMEM((256, 2048), jnp.bfloat16),
            pltpu.VMEM((256, 2048), jnp.bfloat16),
            pltpu.VMEM((TURNS, 256, 256), jnp.float32),
            dma,
            dma,
            dma,
            dma,
            dma,
            dma,
            dma,
            dma((2, 4, TURNS)),
            dma((2, 4, TURNS)),
            dma((TURNS,)),
            dma((TURNS,)),
            dma,
            dma,
            dma((TURNS,)),
            dma((TURNS,)),
            dma,
        ],
        compiler_params=pltpu.CompilerParams(collective_id=0, has_side_effects=True, vmem_limit_bytes=32 << 20),
    )(owner_order, dictionary, residual, coefs, pixel_of)


def maps_kernel(values, pixels, maps, select, parts, state):
    half = 2048

    def spread(q, _):
        points = pl.ds(pl.multiple_of(q * 256, 256), 256)
        ids = pixels[q]
        column = jnp.broadcast_to(ids, (8, 256)).T[:, 0:1] % half
        lane = lax.broadcasted_iota(jnp.int32, (256, 128), 1)
        one = jnp.where(column % 128 == lane, 1.0, 0.0).astype(jnp.bfloat16)
        block = jnp.broadcast_to(column // 128, (256, 128)).astype(jnp.float32).astype(jnp.bfloat16)
        for a in range(16):
            select[points, 128 * a : 128 * (a + 1)] = jnp.where(block == jnp.bfloat16(a), one, jnp.bfloat16(0))
        upper = ids >= half
        for t in range(TURNS):
            v = values[t, :, points]
            high = v.astype(jnp.bfloat16).astype(jnp.float32)
            rest = v - high
            for s, part in enumerate((high, rest)):
                lower_part = jnp.where(upper, 0.0, part).astype(jnp.bfloat16)
                upper_part = jnp.where(upper, part, 0.0).astype(jnp.bfloat16)
                parts[64 * s + 16 * t : 64 * s + 16 * t + 16, points] = lower_part
                parts[128 + 64 * s + 16 * t : 128 + 64 * s + 16 * t + 16, points] = upper_part
        return _

    lax.fori_loop(0, 16, spread, 0)
    for n in range(8):
        cols = slice(256 * n, 256 * (n + 1))
        placed = jnp.dot(parts[...], select[:, cols], preferred_element_type=jnp.float32)
        for h in range(2):
            whole = placed[128 * h : 128 * h + 64] + placed[128 * h + 64 : 128 * h + 128]
            for r in range(2):
                state[16 * h + 2 * n + r] = whole[:, 128 * r : 128 * (r + 1)]

    last = lax.broadcasted_iota(jnp.int32, (32, 8, 128), 2) == 127

    def flow(d):
        scaled = d / edge_scale
        return d / (1.0 + scaled * scaled)

    def smooth(group, _):
        rows = pl.ds(pl.multiple_of(group * 8, 8), 8)
        u = state[:, rows, :]
        for repeat in range(SWEEPS):
            right = jnp.where(last, 0.0, flow(pltpu.roll(u, 127, 2) - u))
            down = flow(u[1:] - u[:-1])
            none = jnp.zeros((1, 8, 128), jnp.float32)
            total = (right - pltpu.roll(right, 1, 2)) + (
                jnp.concatenate([down, none], axis=0) - jnp.concatenate([none, down], axis=0)
            )
            u = u + time_step * total
        for i in range(32):
            maps[rows, i, :] = u[i]
        return _

    lax.fori_loop(0, 8, smooth, 0)


def make_maps(values, pixels):
    vmem = pl.BlockSpec(memory_space=pltpu.VMEM)
    return pl.pallas_call(
        maps_kernel,
        name="make_maps",
        out_shape=jax.ShapeDtypeStruct((64, 32, 128), jnp.float32),
        in_specs=[vmem, vmem],
        out_specs=vmem,
        scratch_shapes=[
            pltpu.VMEM((4096, 2048), jnp.bfloat16),
            pltpu.VMEM((256, 4096), jnp.bfloat16),
            pltpu.VMEM((32, 64, 128), jnp.float32),
        ],
        compiler_params=pltpu.CompilerParams(vmem_limit_bytes=48 << 20),
    )(values, pixels)


def per_device(residual_in, coefs_in, dictionary, owner_order, pixel_of):
    coefs = coefs_in[0].transpose(1, 2, 0)
    values, pixels = unmix(owner_order, dictionary, residual_in[0], coefs, pixel_of)
    return make_maps(values, pixels).reshape(1, TURNS, 16, 32, MAP_W)


def solution(mesh):
    placed = (
        P("field", "point", None),
        P("field", "point", None, None),
        P("field", None),
        P(),
        P("field", "point"),
    )
    return jax.shard_map(
        per_device,
        mesh=mesh,
        in_specs=placed,
        out_specs=P("field", None, "point", None, None),
        check_vma=False,
    )
```

```python
import functools

import jax
import jax.numpy as jnp
from jax import lax
from jax.experimental import pallas as pl
from jax.experimental.pallas import tpu as pltpu
from jax.sharding import PartitionSpec as P

TURNS = 4
SWEEPS = 4
MAP_W = 128
MESH = pl.DeviceIdType.MESH

time_step = 0.2
edge_scale = 0.5


def dev(z, x, core, y):
    return (z // 4 * 8 + x * 2 + core, y * 4 + z % 4)


def remote(src, dst, send, recv, device):
    return pltpu.make_async_remote_copy(
        src_ref=src, dst_ref=dst, send_sem=send, recv_sem=recv, device_id=device, device_id_type=MESH
    )


def nt(a, b):
    return lax.dot_general(a, b, (((1,), (1,)), ((), ())), preferred_element_type=jnp.float32)


def unmix_kernel(
    owner_hbm,
    block,
    residual_hbm,
    coefs_hbm,
    pixel_of,
    maps,
    owner,
    values,
    pixels,
    coefs_in,
    coefs,
    g,
    cand,
    residual,
    templates,
    updated,
    select,
    parts,
    state,
    a_send,
    a_recv,
    b_send,
    b_recv,
    z_send,
    z_recv,
    ring_send,
    ring_recv,
    c_send,
    c_recv,
    id_send,
    id_recv,
    v_send,
    v_recv,
    load_sem,
):
    f = lax.axis_index("field")
    p = lax.axis_index("point")
    core = f % 2
    chip = f // 2
    x = chip % 4
    zh = f // 8
    y = p // 4
    z = zh * 4 + p % 4
    sibling = (f + 1 - 2 * core, p)

    barrier = pltpu.get_barrier_semaphore()

    def greet(device):
        pl.semaphore_signal(barrier, inc=1, device_id=device, device_id_type=MESH)

    def greet_field(i, _):
        greet(((chip + i) % 16 * 2 + core, p))
        return _

    lax.fori_loop(1, 16, greet_field, 0)

    def greet_z(i, _):
        @pl.when(i % 4 != 0)
        def _greet():
            greet(dev((z + i) % 16, x, core, y))

        return _

    lax.fori_loop(1, 16, greet_z, 0)

    def greet_point(i, _):
        to = (p + i) % 16

        @pl.when(to // 4 != y)
        def _greet():
            greet((f, to))

        return _

    lax.fori_loop(1, 16, greet_point, 0)
    greet(sibling)
    lanes = pl.ds(pl.multiple_of(p * 128, 128), 128)

    def tile_of(to):
        return block.at[pl.ds(pl.multiple_of(to * 16, 16), 16), lanes]

    load_own = pltpu.make_async_copy(tile_of(chip), cand.at[core, chip], load_sem.at[0])
    load_owner = pltpu.make_async_copy(owner_hbm, owner, load_sem.at[1])
    load_pixels = pltpu.make_async_copy(pixel_of, pixels.at[p], load_sem.at[2])
    load_coefs = pltpu.make_async_copy(coefs_hbm, coefs_in, load_sem.at[3])
    load_residual = pltpu.make_async_copy(residual_hbm, residual, load_sem.at[4])
    load_own.start()
    load_owner.start()
    load_pixels.start()
    load_coefs.start()
    load_residual.start()
    pl.semaphore_wait(barrier, 15 + 12 + 12 + 1)

    def scatter(i, _):
        to = (chip + 4 * ((i // 4 + 2) % 4) + i % 4) % 16

        @pl.when(to != chip)
        def _send():
            remote(tile_of(to), cand.at[core, chip], a_send, a_recv, (to * 2 + core, p)).start()

        return _

    lax.fori_loop(0, 16, scatter, 0)

    def tell_pixels(i, _):
        remote(pixel_of, pixels.at[p], id_send, id_recv, (f, (p + i) % 16)).start()
        return _

    lax.fori_loop(1, 16, tell_pixels, 0)
    load_own.wait()
    load_owner.wait()
    all_a = remote(cand.at[0, pl.ds(0, 15)], cand.at[0, pl.ds(0, 15)], a_send, a_recv, sibling)
    all_a.wait_recv()
    both = remote(cand.at[core], cand.at[core], b_send, b_recv, sibling)
    both.start()
    all_a.wait_send()
    both.wait()

    mine = pl.ds(pl.multiple_of(x * 16, 16), 16)
    for tt in range(2):
        o = owner[core + 2 * tt]
        g[core, tt, p, zh, mine, :] = cand[o % 2, o // 2]

    def along_z(i, _):
        part = g.at[core, :, p, zh, mine, :]
        step = 8 + (i + 1) // 2 * (1 - i % 2 * 2)
        remote(part, part, z_send, z_recv, dev((z + step) % 16, x, core, y)).start()
        return _

    lax.fori_loop(0, 15, along_z, 0)
    load_coefs.wait()
    for t in range(TURNS):
        coefs[t] = coefs_in[:, t, :].astype(jnp.float32).T
    amount = g.at[0, 0, pl.ds(0, 15), 0, pl.ds(0, 32), :]
    all_z = remote(amount, amount, z_send, z_recv, sibling)
    all_z.wait_recv()
    all_z.wait_send()

    def ring(stage, neighbour, region):
        def make(t, kind):
            offset, half, to = ((0, None, 1), (0, None, 3), (3, 0, 1), (1, 1, 3))[kind]
            ref = g.at[region(t, offset, half)]
            return remote(ref, ref, ring_send.at[stage, kind, t], ring_recv.at[stage, kind, t], neighbour(to))

        def start(t):
            make(t, 0).start()
            make(t, 1).start()

        def forward(t):
            make(t, 0).wait_recv()
            make(t, 2).start()
            make(t, 1).wait_recv()
            make(t, 3).start()

        def finish(t):
            make(t, 2).wait_recv()
            make(t, 3).wait_recv()

        def drain(t):
            for kind in range(4):
                make(t, kind).wait_send()

        return start, forward, finish, drain

    def along(axis):
        def neighbour(step):
            if axis == "x":
                return dev(z, (x + step) % 4, core, y)
            return dev(z, x, core, (y + step) % 4)

        return neighbour

    def mid_region(axis):
        def region(t, offset, half):
            bx = (x + offset) % 4 if axis == "x" else x
            by = (y + offset) % 4 if axis == "y" else y
            points = pl.ds(by * 4, 4) if half is None else pl.ds(by * 4 + 2 * half, 2)
            return (core, t // 2, points, pl.ds(t % 2 * 2, 2), pl.ds(pl.multiple_of(bx * 16, 16), 16), slice(None))

        return region

    def last_region(axis):
        def region(t, offset, half):
            if axis == "x":
                points = pl.ds(0, 16) if half is None else pl.ds(8 * half, 8)
                rows = pl.ds(pl.multiple_of((x + offset) % 4 * 16, 16), 16)
            else:
                by = (y + offset) % 4
                points = pl.ds(by * 4, 4) if half is None else pl.ds(by * 4 + 2 * half, 2)
                rows = slice(None)
            return (core, t // 2, points, pl.ds(t % 2 * 2, 2), rows, slice(None))

        return region

    def swap(t):
        part = g.at[core, t // 2, :, pl.ds(t % 2 * 2, 2)]
        return remote(part, part, c_send.at[t], c_recv.at[t], sibling)

    def rings(first, last):
        return ring(0, along(first), mid_region(first)), ring(1, along(last), last_region(last))

    def by_core(act):
        @pl.when(core == 0)
        def _even():
            act(*rings("y", "x"))

        @pl.when(core == 1)
        def _odd():
            act(*rings("x", "y"))

    def open_mid(mid, last):
        for t in range(TURNS):
            mid[0](t)

    def pass_mid(mid, last):
        for t in range(TURNS):
            mid[1](t)

    def open_last(mid, last):
        for t in range(TURNS):
            mid[2](t)
            last[0](t)

    def share(last, t):
        last[2](t)
        swap(t).start()

    def first_half(mid, last):
        last[1](0)
        last[1](1)
        share(last, 0)
        last[1](2)
        share(last, 1)

    def middle(mid, last):
        last[1](3)
        share(last, 2)

    def second_half(mid, last):
        share(last, 3)

    def close(mid, last):
        for t in range(TURNS):
            mid[3](t)
            last[3](t)

    def send_rows(t, to):
        rows = pl.ds(pl.multiple_of(to * 16, 16), 16)
        points = pl.ds(pl.multiple_of(p * 256, 256), 256)
        return updated.at[t, rows], values.at[t, :, points]

    def turn(t):
        for q in range(16):
            templates[:, 128 * q : 128 * (q + 1)] = g[t % 2, t // 2, q].reshape(256, 128)
        gram = nt(templates[...], templates[...])
        step = 1.0 / jnp.sum(jnp.abs(gram), axis=1, keepdims=True)
        before = coefs[t]
        after = jnp.maximum(before + step * nt(templates[...], residual[...]), 0.0)
        updated[t] = after

        def deliver(i, _):
            to = (p + i) % 16
            src, dst = send_rows(t, to)
            remote(src, dst, v_send.at[t], v_recv.at[t], (f, to)).start()
            return _

        lax.fori_loop(1, 16, deliver, 0)
        rows = pl.ds(pl.multiple_of(p * 16, 16), 16)
        values[t, :, pl.ds(pl.multiple_of(p * 256, 256), 256)] = updated[t, rows, :]
        if t + 1 < TURNS:
            change = (after - before).astype(jnp.bfloat16)
            for q in range(4):
                cols = slice(512 * q, 512 * (q + 1))
                moved = lax.dot_general(
                    change, templates[:, cols], (((0,), (0,)), ((), ())), preferred_element_type=jnp.float32
                )
                residual[:, cols] = (residual[:, cols].astype(jnp.float32) - moved).astype(jnp.bfloat16)

    half = 2048

    def spread(q, _):
        points = pl.ds(pl.multiple_of(q * 256, 256), 256)
        column = jnp.broadcast_to(pixels[q], (8, 256)).T[:, 0:1] % half
        lane = lax.broadcasted_iota(jnp.int32, (256, 128), 1)
        one = jnp.where(column % 128 == lane, 1.0, 0.0).astype(jnp.bfloat16)
        group = jnp.broadcast_to(column // 128, (256, 128)).astype(jnp.float32).astype(jnp.bfloat16)
        for a in range(16):
            select[points, 128 * a : 128 * (a + 1)] = jnp.where(group == jnp.bfloat16(a), one, jnp.bfloat16(0))
        return _

    def split(pair):
        def one(q, _):
            points = pl.ds(pl.multiple_of(q * 256, 256), 256)
            upper = pixels[q] >= half
            for i in range(2):
                v = values[2 * pair + i, :, points]
                high = v.astype(jnp.bfloat16).astype(jnp.float32)
                for s, part in enumerate((high, v - high)):
                    row = 32 * s + 16 * i
                    parts[row : row + 16, points] = jnp.where(upper, 0.0, part).astype(jnp.bfloat16)
                    parts[64 + row : 64 + row + 16, points] = jnp.where(upper, part, 0.0).astype(jnp.bfloat16)
            return _

        lax.fori_loop(0, 16, one, 0)

    def place(pair):
        def one(n, _):
            cols = pl.ds(pl.multiple_of(n * 256, 256), 256)
            placed = jnp.dot(parts[...], select[:, cols], preferred_element_type=jnp.float32)
            for h in range(2):
                whole = placed[64 * h : 64 * h + 32] + placed[64 * h + 32 : 64 * h + 64]
                for r in range(2):
                    state[16 * h + 2 * n + r, 32 * pair : 32 * pair + 32] = whole[:, 128 * r : 128 * (r + 1)]
            return _

        lax.fori_loop(0, 8, one, 0)

    def flow(d):
        scaled = d / edge_scale
        return d / (1.0 + scaled * scaled)

    def smooth(group, _):
        last = lax.broadcasted_iota(jnp.int32, (32, 8, 128), 2) == 127
        rows = pl.ds(pl.multiple_of(group * 8, 8), 8)
        u = state[:, rows, :]
        for repeat in range(SWEEPS):
            right = jnp.where(last, 0.0, flow(pltpu.roll(u, 127, 2) - u))
            down = flow(u[1:] - u[:-1])
            none = jnp.zeros((1, 8, 128), jnp.float32)
            total = (right - pltpu.roll(right, 1, 2)) + (
                jnp.concatenate([down, none], axis=0) - jnp.concatenate([none, down], axis=0)
            )
            u = u + time_step * total
        for i in range(32):
            maps[rows, i, :] = u[i]
        return _

    by_core(open_mid)
    ids = remote(pixels.at[pl.ds(0, 15)], pixels.at[pl.ds(0, 15)], id_send, id_recv, sibling)
    load_pixels.wait()
    ids.wait_recv()
    lax.fori_loop(0, 4, spread, 0)
    by_core(pass_mid)
    lax.fori_loop(4, 8, spread, 0)
    by_core(open_last)
    lax.fori_loop(8, 16, spread, 0)
    load_residual.wait()
    by_core(first_half)
    swap(0).wait_recv()
    swap(1).wait_recv()
    turn(0)
    by_core(middle)
    turn(1)
    by_core(second_half)
    swap(2).wait_recv()
    swap(3).wait_recv()
    turn(2)
    turn(3)

    def arrived(t):
        amount = values.at[t, :, pl.ds(0, 15 * 256)]
        remote(amount, amount, v_send.at[t], v_recv.at[t], sibling).wait_recv()

    for pair in range(2):
        arrived(2 * pair)
        arrived(2 * pair + 1)
        split(pair)
        place(pair)
        lax.fori_loop(4 * pair, 4 * pair + 4, smooth, 0)
    by_core(close)
    ids.wait_send()
    for t in range(TURNS):
        swap(t).wait_send()
        amount = values.at[t, :, pl.ds(0, 15 * 256)]
        remote(amount, amount, v_send.at[t], v_recv.at[t], sibling).wait_send()


def unmix(owner_order, dictionary, residual, coefs, pixel_of):
    hbm = pl.BlockSpec(memory_space=pltpu.HBM)
    dma = pltpu.SemaphoreType.DMA
    return pl.pallas_call(
        unmix_kernel,
        name="unmix",
        out_shape=jax.ShapeDtypeStruct((64, 32, 128), jnp.float32),
        in_specs=[hbm] * 5,
        out_specs=pl.BlockSpec(memory_space=pltpu.VMEM),
        scratch_shapes=[
            pltpu.SMEM((32,), jnp.int32),
            pltpu.VMEM((TURNS, 16, 4096), jnp.float32),
            pltpu.VMEM((16, 1, 256), jnp.int32),
            pltpu.VMEM((256, TURNS, 256), jnp.bfloat16),
            pltpu.VMEM((TURNS, 256, 256), jnp.float32),
            pltpu.VMEM((2, 2, 16, 4, 64, 128), jnp.bfloat16),
            pltpu.VMEM((2, 16, 16, 128), jnp.bfloat16),
            pltpu.VMEM((256, 2048), jnp.bfloat16),
            pltpu.VMEM((256, 2048), jnp.bfloat16),
            pltpu.VMEM((TURNS, 256, 256), jnp.float32),
            pltpu.VMEM((4096, 2048), jnp.bfloat16),
            pltpu.VMEM((128, 4096), jnp.bfloat16),
            pltpu.VMEM((32, 64, 128), jnp.float32),
            dma,
            dma,
            dma,
            dma,
            dma,
            dma,
            dma((2, 4, TURNS)),
            dma((2, 4, TURNS)),
            dma((TURNS,)),
            dma((TURNS,)),
            dma,
            dma,
            dma((TURNS,)),
            dma((TURNS,)),
            dma((5,)),
        ],
        compiler_params=pltpu.CompilerParams(collective_id=0, has_side_effects=True, vmem_limit_bytes=48 << 20),
    )(owner_order, dictionary, residual, coefs, pixel_of)


def per_device(residual_in, coefs_in, dictionary, owner_order, pixel_of):
    maps = unmix(owner_order, dictionary, residual_in[0], coefs_in[0], pixel_of)
    return maps.reshape(1, TURNS, 16, 32, MAP_W)


def solution(mesh):
    placed = (
        P("field", "point", None),
        P("field", "point", None, None),
        P("field", None),
        P(),
        P("field", "point"),
    )
    return jax.shard_map(
        per_device,
        mesh=mesh,
        in_specs=placed,
        out_specs=P("field", None, "point", None, None),
        check_vma=False,
    )
```

```python
import functools

import jax
import jax.numpy as jnp
from jax import lax
from jax.experimental import pallas as pl
from jax.experimental.pallas import tpu as pltpu
from jax.sharding import PartitionSpec as P

TURNS = 4
SWEEPS = 4
MAP_W = 128
MESH = pl.DeviceIdType.MESH
LEVELS = 65534.0

time_step = 0.2
edge_scale = 0.5


def dev(z, x, core, y):
    return (z // 4 * 8 + x * 2 + core, y * 4 + z % 4)


def remote(src, dst, send, recv, device):
    return pltpu.make_async_remote_copy(
        src_ref=src, dst_ref=dst, send_sem=send, recv_sem=recv, device_id=device, device_id_type=MESH
    )


def nt(a, b):
    return lax.dot_general(a, b, (((1,), (1,)), ((), ())), preferred_element_type=jnp.float32)


def unmix_kernel(
    owner_hbm,
    block,
    residual_hbm,
    coefs_hbm,
    pixel_of,
    maps,
    owner,
    codes,
    peaks,
    peak_cols,
    pixels,
    coefs_in,
    coefs,
    g,
    cand,
    residual,
    templates,
    updated,
    select,
    parts,
    state,
    a_send,
    a_recv,
    b_send,
    b_recv,
    z_send,
    z_recv,
    ring_send,
    ring_recv,
    c_send,
    c_recv,
    id_send,
    id_recv,
    v_send,
    v_recv,
    s_send,
    s_recv,
    load_sem,
):
    f = lax.axis_index("field")
    p = lax.axis_index("point")
    core = f % 2
    chip = f // 2
    x = chip % 4
    zh = f // 8
    y = p // 4
    z = zh * 4 + p % 4
    sibling = (f + 1 - 2 * core, p)

    barrier = pltpu.get_barrier_semaphore()

    def greet(device):
        pl.semaphore_signal(barrier, inc=1, device_id=device, device_id_type=MESH)

    def greet_field(i, _):
        greet(((chip + i) % 16 * 2 + core, p))
        return _

    lax.fori_loop(1, 16, greet_field, 0)

    def greet_z(i, _):
        @pl.when(i % 4 != 0)
        def _greet():
            greet(dev((z + i) % 16, x, core, y))

        return _

    lax.fori_loop(1, 16, greet_z, 0)

    def greet_point(i, _):
        to = (p + i) % 16

        @pl.when(to // 4 != y)
        def _greet():
            greet((f, to))

        return _

    lax.fori_loop(1, 16, greet_point, 0)
    greet(sibling)
    lanes = pl.ds(pl.multiple_of(p * 128, 128), 128)

    def tile_of(to):
        return block.at[pl.ds(pl.multiple_of(to * 16, 16), 16), lanes]

    load_own = pltpu.make_async_copy(tile_of(chip), cand.at[core, chip], load_sem.at[0])
    load_owner = pltpu.make_async_copy(owner_hbm, owner, load_sem.at[1])
    load_pixels = pltpu.make_async_copy(pixel_of, pixels.at[p], load_sem.at[2])
    load_coefs = pltpu.make_async_copy(coefs_hbm, coefs_in, load_sem.at[3])
    load_residual = pltpu.make_async_copy(residual_hbm, residual, load_sem.at[4])
    load_own.start()
    load_owner.start()
    load_pixels.start()
    load_coefs.start()
    load_residual.start()
    pl.semaphore_wait(barrier, 15 + 12 + 12 + 1)

    def scatter(i, _):
        to = (chip + 4 * ((i // 4 + 2) % 4) + i % 4) % 16

        @pl.when(to != chip)
        def _send():
            remote(tile_of(to), cand.at[core, chip], a_send, a_recv, (to * 2 + core, p)).start()

        return _

    lax.fori_loop(0, 16, scatter, 0)

    def tell_pixels(i, _):
        remote(pixel_of, pixels.at[p], id_send, id_recv, (f, (p + i) % 16)).start()
        return _

    lax.fori_loop(1, 16, tell_pixels, 0)
    load_own.wait()
    load_owner.wait()
    all_a = remote(cand.at[0, pl.ds(0, 15)], cand.at[0, pl.ds(0, 15)], a_send, a_recv, sibling)
    all_a.wait_recv()
    both = remote(cand.at[core], cand.at[core], b_send, b_recv, sibling)
    both.start()
    all_a.wait_send()
    both.wait()

    mine = pl.ds(pl.multiple_of(x * 16, 16), 16)
    for tt in range(2):
        o = owner[core + 2 * tt]
        g[core, tt, p, zh, mine, :] = cand[o % 2, o // 2]

    def along_z(i, _):
        part = g.at[core, :, p, zh, mine, :]
        step = 8 + (i + 1) // 2 * (1 - i % 2 * 2)
        remote(part, part, z_send, z_recv, dev((z + step) % 16, x, core, y)).start()
        return _

    lax.fori_loop(0, 15, along_z, 0)
    load_coefs.wait()
    for t in range(TURNS):
        coefs[t] = coefs_in[:, t, :].astype(jnp.float32).T
    amount = g.at[0, 0, pl.ds(0, 15), 0, pl.ds(0, 32), :]
    all_z = remote(amount, amount, z_send, z_recv, sibling)
    all_z.wait_recv()
    all_z.wait_send()

    def ring(stage, neighbour, region):
        def make(t, kind):
            offset, half, to = ((0, None, 1), (0, None, 3), (3, 0, 1), (1, 1, 3))[kind]
            ref = g.at[region(t, offset, half)]
            return remote(ref, ref, ring_send.at[stage, kind, t], ring_recv.at[stage, kind, t], neighbour(to))

        def start(t):
            make(t, 0).start()
            make(t, 1).start()

        def forward(t):
            make(t, 0).wait_recv()
            make(t, 2).start()
            make(t, 1).wait_recv()
            make(t, 3).start()

        def finish(t):
            make(t, 2).wait_recv()
            make(t, 3).wait_recv()

        def drain(t):
            for kind in range(4):
                make(t, kind).wait_send()

        return start, forward, finish, drain

    def along(axis):
        def neighbour(step):
            if axis == "x":
                return dev(z, (x + step) % 4, core, y)
            return dev(z, x, core, (y + step) % 4)

        return neighbour

    def mid_region(axis):
        def region(t, offset, half):
            bx = (x + offset) % 4 if axis == "x" else x
            by = (y + offset) % 4 if axis == "y" else y
            points = pl.ds(by * 4, 4) if half is None else pl.ds(by * 4 + 2 * half, 2)
            return (core, t // 2, points, pl.ds(t % 2 * 2, 2), pl.ds(pl.multiple_of(bx * 16, 16), 16), slice(None))

        return region

    def last_region(axis):
        def region(t, offset, half):
            if axis == "x":
                points = pl.ds(0, 16) if half is None else pl.ds(8 * half, 8)
                rows = pl.ds(pl.multiple_of((x + offset) % 4 * 16, 16), 16)
            else:
                by = (y + offset) % 4
                points = pl.ds(by * 4, 4) if half is None else pl.ds(by * 4 + 2 * half, 2)
                rows = slice(None)
            return (core, t // 2, points, pl.ds(t % 2 * 2, 2), rows, slice(None))

        return region

    def swap(t):
        part = g.at[core, t // 2, :, pl.ds(t % 2 * 2, 2)]
        return remote(part, part, c_send.at[t], c_recv.at[t], sibling)

    def rings(first, last):
        return ring(0, along(first), mid_region(first)), ring(1, along(last), last_region(last))

    def by_core(act):
        @pl.when(core == 0)
        def _even():
            act(*rings("y", "x"))

        @pl.when(core == 1)
        def _odd():
            act(*rings("x", "y"))

    def open_mid(mid, last):
        for t in range(TURNS):
            mid[0](t)

    def pass_mid(mid, last):
        for t in range(TURNS):
            mid[1](t)

    def open_last(mid, last):
        for t in range(TURNS):
            mid[2](t)
            last[0](t)

    def share(last, t):
        last[2](t)
        swap(t).start()

    def first_half(mid, last):
        last[1](0)
        last[1](1)
        share(last, 0)
        last[1](2)
        share(last, 1)

    def middle(mid, last):
        last[1](3)
        share(last, 2)

    def second_half(mid, last):
        share(last, 3)

    def close(mid, last):
        for t in range(TURNS):
            mid[3](t)
            last[3](t)

    def send_rows(t, to):
        rows = pl.ds(pl.multiple_of(to * 16, 16), 16)
        points = pl.ds(pl.multiple_of(p * 256, 256), 256)
        return updated.at[t, rows], codes.at[t, :, points]

    def turn(t):
        for q in range(16):
            templates[:, 128 * q : 128 * (q + 1)] = g[t % 2, t // 2, q].reshape(256, 128)
        gram = nt(templates[...], templates[...])
        step = 1.0 / jnp.sum(jnp.abs(gram), axis=1, keepdims=True)
        before = coefs[t]
        after = jnp.maximum(before + step * nt(templates[...], residual[...]), 0.0)
        peak = jnp.max(after, axis=1, keepdims=True)
        share_of_peak = after / jnp.where(peak > 0.0, peak, 1.0)
        updated[t] = (jnp.floor(share_of_peak * LEVELS + 0.5) - LEVELS / 2).astype(jnp.int32).astype(jnp.int16)
        peaks[t, p] = jnp.broadcast_to(peak, (256, 128)).T[0:1]

        def deliver(i, _):
            to = (p + i) % 16
            src, dst = send_rows(t, to)
            remote(src, dst, v_send.at[t], v_recv.at[t], (f, to)).start()
            remote(peaks.at[t, p], peaks.at[t, p], s_send.at[t], s_recv.at[t], (f, to)).start()
            return _

        lax.fori_loop(1, 16, deliver, 0)
        rows = pl.ds(pl.multiple_of(p * 16, 16), 16)
        codes[t, :, pl.ds(pl.multiple_of(p * 256, 256), 256)] = updated[t, rows, :]
        if t + 1 < TURNS:
            change = (after - before).astype(jnp.bfloat16)
            for q in range(4):
                cols = slice(512 * q, 512 * (q + 1))
                moved = lax.dot_general(
                    change, templates[:, cols], (((0,), (0,)), ((), ())), preferred_element_type=jnp.float32
                )
                residual[:, cols] = (residual[:, cols].astype(jnp.float32) - moved).astype(jnp.bfloat16)

    half = 2048

    def spread(q, _):
        points = pl.ds(pl.multiple_of(q * 256, 256), 256)
        column = jnp.broadcast_to(pixels[q], (8, 256)).T[:, 0:1] % half
        lane = lax.broadcasted_iota(jnp.int32, (256, 128), 1)
        one = jnp.where(column % 128 == lane, 1.0, 0.0).astype(jnp.bfloat16)
        group = jnp.broadcast_to(column // 128, (256, 128)).astype(jnp.float32).astype(jnp.bfloat16)
        for a in range(16):
            select[points, 128 * a : 128 * (a + 1)] = jnp.where(group == jnp.bfloat16(a), one, jnp.bfloat16(0))
        return _

    def split(t):
        peak_cols[:, 0:16] = peaks[t].reshape(16, 256).T
        own_peaks = peak_cols[pl.ds(pl.multiple_of(p * 16, 16), 16), :] * (1.0 / LEVELS)
        source = lax.broadcasted_iota(jnp.int32, (16, 128), 1)

        def one(q, _):
            points = pl.ds(pl.multiple_of(q * 256, 256), 256)
            upper = pixels[q] >= half
            scale = jnp.sum(jnp.where(source == q, own_peaks, 0.0), axis=1, keepdims=True)
            v = (codes[t, :, points].astype(jnp.int32).astype(jnp.float32) + LEVELS / 2) * scale
            high = v.astype(jnp.bfloat16).astype(jnp.float32)
            for s, part in enumerate((high, v - high)):
                row = 32 * s + t % 2 * 16
                parts[row : row + 16, points] = jnp.where(upper, 0.0, part).astype(jnp.bfloat16)
                parts[64 + row : 64 + row + 16, points] = jnp.where(upper, part, 0.0).astype(jnp.bfloat16)
            return _

        lax.fori_loop(0, 16, one, 0)

    def place(pair):
        def one(n, _):
            cols = pl.ds(pl.multiple_of(n * 256, 256), 256)
            placed = jnp.dot(parts[...], select[:, cols], preferred_element_type=jnp.float32)
            for h in range(2):
                whole = placed[64 * h : 64 * h + 32] + placed[64 * h + 32 : 64 * h + 64]
                for r in range(2):
                    state[16 * h + 2 * n + r, 32 * pair : 32 * pair + 32] = whole[:, 128 * r : 128 * (r + 1)]
            return _

        lax.fori_loop(0, 8, one, 0)

    def flow(d):
        scaled = d * (1.0 / edge_scale)
        return d / (1.0 + scaled * scaled)

    def smooth(group, _):
        last = lax.broadcasted_iota(jnp.int32, (32, 8, 128), 2) == 127
        rows = pl.ds(pl.multiple_of(group * 8, 8), 8)
        u = state[:, rows, :]
        for repeat in range(SWEEPS):
            right = jnp.where(last, 0.0, flow(pltpu.roll(u, 127, 2) - u))
            down = flow(u[1:] - u[:-1])
            none = jnp.zeros((1, 8, 128), jnp.float32)
            total = (right - pltpu.roll(right, 1, 2)) + (
                jnp.concatenate([down, none], axis=0) - jnp.concatenate([none, down], axis=0)
            )
            u = u + time_step * total
        for i in range(32):
            maps[rows, i, :] = u[i]
        return _

    by_core(open_mid)
    ids = remote(pixels.at[pl.ds(0, 15)], pixels.at[pl.ds(0, 15)], id_send, id_recv, sibling)
    load_pixels.wait()
    ids.wait_recv()
    lax.fori_loop(0, 4, spread, 0)
    by_core(pass_mid)
    lax.fori_loop(4, 8, spread, 0)
    by_core(open_last)
    lax.fori_loop(8, 16, spread, 0)
    load_residual.wait()
    by_core(first_half)
    swap(0).wait_recv()
    swap(1).wait_recv()
    turn(0)
    by_core(middle)
    turn(1)
    by_core(second_half)
    swap(2).wait_recv()
    swap(3).wait_recv()
    turn(2)
    turn(3)

    def sent(t):
        amount = codes.at[t, :, pl.ds(0, 15 * 256)]
        rows = peaks.at[t, pl.ds(0, 15)]
        return (
            remote(amount, amount, v_send.at[t], v_recv.at[t], sibling),
            remote(rows, rows, s_send.at[t], s_recv.at[t], sibling),
        )

    for pair in range(2):
        for t in (2 * pair, 2 * pair + 1):
            for copies in sent(t):
                copies.wait_recv()
            split(t)
        place(pair)
        lax.fori_loop(4 * pair, 4 * pair + 4, smooth, 0)
    by_core(close)
    ids.wait_send()
    for t in range(TURNS):
        swap(t).wait_send()
        for copies in sent(t):
            copies.wait_send()


def unmix(owner_order, dictionary, residual, coefs, pixel_of):
    hbm = pl.BlockSpec(memory_space=pltpu.HBM)
    dma = pltpu.SemaphoreType.DMA
    return pl.pallas_call(
        unmix_kernel,
        name="unmix",
        out_shape=jax.ShapeDtypeStruct((64, 32, 128), jnp.float32),
        in_specs=[hbm] * 5,
        out_specs=pl.BlockSpec(memory_space=pltpu.VMEM),
        scratch_shapes=[
            pltpu.SMEM((32,), jnp.int32),
            pltpu.VMEM((TURNS, 16, 4096), jnp.int16),
            pltpu.VMEM((TURNS, 16, 1, 256), jnp.float32),
            pltpu.VMEM((256, 128), jnp.float32),
            pltpu.VMEM((16, 1, 256), jnp.int32),
            pltpu.VMEM((256, TURNS, 256), jnp.bfloat16),
            pltpu.VMEM((TURNS, 256, 256), jnp.float32),
            pltpu.VMEM((2, 2, 16, 4, 64, 128), jnp.bfloat16),
            pltpu.VMEM((2, 16, 16, 128), jnp.bfloat16),
            pltpu.VMEM((256, 2048), jnp.bfloat16),
            pltpu.VMEM((256, 2048), jnp.bfloat16),
            pltpu.VMEM((TURNS, 256, 256), jnp.int16),
            pltpu.VMEM((4096, 2048), jnp.bfloat16),
            pltpu.VMEM((128, 4096), jnp.bfloat16),
            pltpu.VMEM((32, 64, 128), jnp.float32),
            dma,
            dma,
            dma,
            dma,
            dma,
            dma,
            dma((2, 4, TURNS)),
            dma((2, 4, TURNS)),
            dma((TURNS,)),
            dma((TURNS,)),
            dma,
            dma,
            dma((TURNS,)),
            dma((TURNS,)),
            dma((TURNS,)),
            dma((TURNS,)),
            dma((5,)),
        ],
        compiler_params=pltpu.CompilerParams(collective_id=0, has_side_effects=True, vmem_limit_bytes=60 << 20),
    )(owner_order, dictionary, residual, coefs, pixel_of)


def per_device(residual_in, coefs_in, dictionary, owner_order, pixel_of):
    maps = unmix(owner_order, dictionary, residual_in[0], coefs_in[0], pixel_of)
    return maps.reshape(1, TURNS, 16, 32, MAP_W)


def solution(mesh):
    placed = (
        P("field", "point", None),
        P("field", "point", None, None),
        P("field", None),
        P(),
        P("field", "point"),
    )
    return jax.shard_map(
        per_device,
        mesh=mesh,
        in_specs=placed,
        out_specs=P("field", None, "point", None, None),
        check_vma=False,
    )
```

```python
import functools

import jax
import jax.numpy as jnp
from jax import lax
from jax.experimental import pallas as pl
from jax.experimental.pallas import tpu as pltpu
from jax.sharding import PartitionSpec as P

TURNS = 4
SWEEPS = 4
MAP_W = 128
MESH = pl.DeviceIdType.MESH
LEVELS = 65534.0
GROUPS = 8
SPAN = 4096 // GROUPS

time_step = 0.2
edge_scale = 0.5


def dev(z, x, core, y):
    return (z // 4 * 8 + x * 2 + core, y * 4 + z % 4)


def remote(src, dst, send, recv, device):
    return pltpu.make_async_remote_copy(
        src_ref=src, dst_ref=dst, send_sem=send, recv_sem=recv, device_id=device, device_id_type=MESH
    )


def nt(a, b):
    return lax.dot_general(a, b, (((1,), (1,)), ((), ())), preferred_element_type=jnp.float32)


def unmix_kernel(
    owner_hbm,
    block,
    residual_hbm,
    coefs_hbm,
    pixel_of,
    maps,
    owner,
    codes,
    peaks,
    peak_cols,
    pixels,
    coefs_in,
    coefs,
    g,
    cand,
    residual,
    templates,
    updated,
    member,
    select,
    parts,
    state,
    a_send,
    a_recv,
    b_send,
    b_recv,
    z_send,
    z_recv,
    ring_send,
    ring_recv,
    c_send,
    c_recv,
    id_send,
    id_recv,
    v_send,
    v_recv,
    s_send,
    s_recv,
    load_sem,
):
    f = lax.axis_index("field")
    p = lax.axis_index("point")
    core = f % 2
    chip = f // 2
    x = chip % 4
    zh = f // 8
    y = p // 4
    z = zh * 4 + p % 4
    sibling = (f + 1 - 2 * core, p)

    barrier = pltpu.get_barrier_semaphore()

    def greet(device):
        pl.semaphore_signal(barrier, inc=1, device_id=device, device_id_type=MESH)

    def greet_field(i, _):
        greet(((chip + i) % 16 * 2 + core, p))
        return _

    lax.fori_loop(1, 16, greet_field, 0)

    def greet_z(i, _):
        @pl.when(i % 4 != 0)
        def _greet():
            greet(dev((z + i) % 16, x, core, y))

        return _

    lax.fori_loop(1, 16, greet_z, 0)

    def greet_point(i, _):
        to = (p + i) % 16

        @pl.when(to // 4 != y)
        def _greet():
            greet((f, to))

        return _

    lax.fori_loop(1, 16, greet_point, 0)
    greet(sibling)
    lanes = pl.ds(pl.multiple_of(p * 128, 128), 128)

    def tile_of(to):
        return block.at[pl.ds(pl.multiple_of(to * 16, 16), 16), lanes]

    load_own = pltpu.make_async_copy(tile_of(chip), cand.at[core, chip], load_sem.at[0])
    load_owner = pltpu.make_async_copy(owner_hbm, owner, load_sem.at[1])
    load_pixels = pltpu.make_async_copy(pixel_of, pixels.at[p], load_sem.at[2])
    load_coefs = pltpu.make_async_copy(coefs_hbm, coefs_in, load_sem.at[3])
    load_residual = pltpu.make_async_copy(residual_hbm, residual, load_sem.at[4])
    load_own.start()
    load_owner.start()
    load_pixels.start()
    load_coefs.start()
    load_residual.start()
    pl.semaphore_wait(barrier, 15 + 12 + 12 + 1)

    def scatter(i, _):
        to = (chip + 4 * ((i // 4 + 2) % 4) + i % 4) % 16

        @pl.when(to != chip)
        def _send():
            remote(tile_of(to), cand.at[core, chip], a_send, a_recv, (to * 2 + core, p)).start()

        return _

    lax.fori_loop(0, 16, scatter, 0)

    def tell_pixels(i, _):
        remote(pixel_of, pixels.at[p], id_send, id_recv, (f, (p + i) % 16)).start()
        return _

    lax.fori_loop(1, 16, tell_pixels, 0)
    load_own.wait()
    load_owner.wait()
    all_a = remote(cand.at[0, pl.ds(0, 15)], cand.at[0, pl.ds(0, 15)], a_send, a_recv, sibling)
    all_a.wait_recv()
    both = remote(cand.at[core], cand.at[core], b_send, b_recv, sibling)
    both.start()
    all_a.wait_send()
    both.wait()

    mine = pl.ds(pl.multiple_of(x * 16, 16), 16)
    for tt in range(2):
        o = owner[core + 2 * tt]
        g[core, tt, p, zh, mine, :] = cand[o % 2, o // 2]

    def along_z(i, _):
        part = g.at[core, :, p, zh, mine, :]
        step = 8 + (i + 1) // 2 * (1 - i % 2 * 2)
        remote(part, part, z_send, z_recv, dev((z + step) % 16, x, core, y)).start()
        return _

    lax.fori_loop(0, 15, along_z, 0)
    load_coefs.wait()
    for t in range(TURNS):
        coefs[t] = coefs_in[:, t, :].astype(jnp.float32).T
    amount = g.at[0, 0, pl.ds(0, 15), 0, pl.ds(0, 32), :]
    all_z = remote(amount, amount, z_send, z_recv, sibling)
    all_z.wait_recv()
    all_z.wait_send()

    def ring(stage, neighbour, region):
        def make(t, kind):
            offset, half, to = ((0, None, 1), (0, None, 3), (3, 0, 1), (1, 1, 3))[kind]
            ref = g.at[region(t, offset, half)]
            return remote(ref, ref, ring_send.at[stage, kind, t], ring_recv.at[stage, kind, t], neighbour(to))

        def start(t):
            make(t, 0).start()
            make(t, 1).start()

        def forward(t):
            make(t, 0).wait_recv()
            make(t, 2).start()
            make(t, 1).wait_recv()
            make(t, 3).start()

        def finish(t):
            make(t, 2).wait_recv()
            make(t, 3).wait_recv()

        def drain(t):
            for kind in range(4):
                make(t, kind).wait_send()

        return start, forward, finish, drain

    def along(axis):
        def neighbour(step):
            if axis == "x":
                return dev(z, (x + step) % 4, core, y)
            return dev(z, x, core, (y + step) % 4)

        return neighbour

    def mid_region(axis):
        def region(t, offset, half):
            bx = (x + offset) % 4 if axis == "x" else x
            by = (y + offset) % 4 if axis == "y" else y
            points = pl.ds(by * 4, 4) if half is None else pl.ds(by * 4 + 2 * half, 2)
            return (core, t // 2, points, pl.ds(t % 2 * 2, 2), pl.ds(pl.multiple_of(bx * 16, 16), 16), slice(None))

        return region

    def last_region(axis):
        def region(t, offset, half):
            if axis == "x":
                points = pl.ds(0, 16) if half is None else pl.ds(8 * half, 8)
                rows = pl.ds(pl.multiple_of((x + offset) % 4 * 16, 16), 16)
            else:
                by = (y + offset) % 4
                points = pl.ds(by * 4, 4) if half is None else pl.ds(by * 4 + 2 * half, 2)
                rows = slice(None)
            return (core, t // 2, points, pl.ds(t % 2 * 2, 2), rows, slice(None))

        return region

    def swap(t):
        part = g.at[core, t // 2, :, pl.ds(t % 2 * 2, 2)]
        return remote(part, part, c_send.at[t], c_recv.at[t], sibling)

    def rings(first, last):
        return ring(0, along(first), mid_region(first)), ring(1, along(last), last_region(last))

    def by_core(act):
        @pl.when(core == 0)
        def _even():
            act(*rings("y", "x"))

        @pl.when(core == 1)
        def _odd():
            act(*rings("x", "y"))

    def open_mid(mid, last):
        for t in range(TURNS):
            mid[0](t)

    def pass_mid(mid, last):
        for t in range(TURNS):
            mid[1](t)

    def open_last(mid, last):
        for t in range(TURNS):
            mid[2](t)
            if t < 2:
                last[0](t)

    def share(last, t):
        last[2](t)
        swap(t).start()

    def first_half(mid, last):
        last[1](0)
        last[0](2)
        last[1](1)
        last[0](3)
        share(last, 0)
        last[1](2)
        share(last, 1)

    def middle(mid, last):
        last[1](3)
        share(last, 2)

    def second_half(mid, last):
        share(last, 3)

    def close(mid, last):
        for t in range(TURNS):
            mid[3](t)
            last[3](t)

    def send_rows(t, to):
        rows = pl.ds(pl.multiple_of(to * 16, 16), 16)
        points = pl.ds(pl.multiple_of(p * 256, 256), 256)
        return updated.at[t, rows], codes.at[t, :, points]

    def turn(t):
        for q in range(16):
            templates[:, 128 * q : 128 * (q + 1)] = g[t % 2, t // 2, q].reshape(256, 128)
        gram = nt(templates[...], templates[...])
        step = 1.0 / jnp.sum(jnp.abs(gram), axis=1, keepdims=True)
        before = coefs[t]
        after = jnp.maximum(before + step * nt(templates[...], residual[...]), 0.0)
        peak = jnp.max(after, axis=1, keepdims=True)
        share_of_peak = after / jnp.where(peak > 0.0, peak, 1.0)
        updated[t] = (jnp.floor(share_of_peak * LEVELS + 0.5) - LEVELS / 2).astype(jnp.int32).astype(jnp.int16)
        peaks[t, p] = jnp.broadcast_to(peak, (256, 128)).T[0:1]

        def deliver(i, _):
            to = (p + i) % 16
            src, dst = send_rows(t, to)
            remote(src, dst, v_send.at[t], v_recv.at[t], (f, to)).start()
            remote(peaks.at[t, p], peaks.at[t, p], s_send.at[t], s_recv.at[t], (f, to)).start()
            return _

        lax.fori_loop(1, 16, deliver, 0)
        rows = pl.ds(pl.multiple_of(p * 16, 16), 16)
        codes[t, :, pl.ds(pl.multiple_of(p * 256, 256), 256)] = updated[t, rows, :]
        if t + 1 < TURNS:
            change = (after - before).astype(jnp.bfloat16)
            for q in range(4):
                cols = slice(512 * q, 512 * (q + 1))
                moved = lax.dot_general(
                    change, templates[:, cols], (((0,), (0,)), ((), ())), preferred_element_type=jnp.float32
                )
                residual[:, cols] = (residual[:, cols].astype(jnp.float32) - moved).astype(jnp.bfloat16)

    def spread(q, _):
        points = pl.ds(pl.multiple_of(q * 256, 256), 256)
        ids = pixels[q]
        for h in range(GROUPS):
            here = jnp.where(ids // SPAN == h, 1.0, 0.0)
            member[16 * h : 16 * h + 16, points] = jnp.broadcast_to(here, (16, 256)).astype(jnp.bfloat16)
        column = jnp.broadcast_to(ids, (8, 256)).T[:, 0:1] % SPAN
        lane = lax.broadcasted_iota(jnp.int32, (256, SPAN), 1)
        select[points, :] = jnp.where(column == lane, 1.0, 0.0).astype(jnp.bfloat16)
        return _

    def split(t):
        peak_cols[:, 0:16] = peaks[t].reshape(16, 256).T
        own_peaks = peak_cols[pl.ds(pl.multiple_of(p * 16, 16), 16), :] * (1.0 / LEVELS)
        source = lax.broadcasted_iota(jnp.int32, (16, 128), 1)

        def one(q, _):
            points = pl.ds(pl.multiple_of(q * 256, 256), 256)
            scale = jnp.sum(jnp.where(source == q, own_peaks, 0.0), axis=1, keepdims=True)
            v = (codes[t, :, points].astype(jnp.int32).astype(jnp.float32) + LEVELS / 2) * scale
            high = v.astype(jnp.bfloat16)
            rest = (v - high.astype(jnp.float32)).astype(jnp.bfloat16)
            for h in range(GROUPS):
                here = member[16 * h : 16 * h + 16, points]
                parts[32 * h : 32 * h + 16, points] = high * here
                parts[32 * h + 16 : 32 * h + 32, points] = rest * here
            return _

        lax.fori_loop(0, 16, one, 0)

    def place(t):
        for n in range(SPAN // 256):
            placed = jnp.dot(
                parts[...], select[:, 256 * n : 256 * (n + 1)], preferred_element_type=jnp.float32
            )
            for h in range(GROUPS):
                whole = placed[32 * h : 32 * h + 16] + placed[32 * h + 16 : 32 * h + 32]
                for r in range(2):
                    row = h * (SPAN // 128) + 2 * n + r
                    state[row, 16 * t : 16 * t + 16] = whole[:, 128 * r : 128 * (r + 1)]

    def flow(d):
        scaled = d * (1.0 / edge_scale)
        return d / (1.0 + scaled * scaled)

    def smooth(group, _):
        last = lax.broadcasted_iota(jnp.int32, (32, 8, 128), 2) == 127
        rows = pl.ds(pl.multiple_of(group * 8, 8), 8)
        u = state[:, rows, :]
        for repeat in range(SWEEPS):
            right = jnp.where(last, 0.0, flow(pltpu.roll(u, 127, 2) - u))
            down = flow(u[1:] - u[:-1])
            none = jnp.zeros((1, 8, 128), jnp.float32)
            total = (right - pltpu.roll(right, 1, 2)) + (
                jnp.concatenate([down, none], axis=0) - jnp.concatenate([none, down], axis=0)
            )
            u = u + time_step * total
        for i in range(32):
            maps[rows, i, :] = u[i]
        return _

    by_core(open_mid)
    ids = remote(pixels.at[pl.ds(0, 15)], pixels.at[pl.ds(0, 15)], id_send, id_recv, sibling)
    load_pixels.wait()
    ids.wait_recv()
    lax.fori_loop(0, 4, spread, 0)
    by_core(pass_mid)
    lax.fori_loop(4, 8, spread, 0)
    by_core(open_last)
    lax.fori_loop(8, 16, spread, 0)
    load_residual.wait()
    by_core(first_half)
    swap(0).wait_recv()
    swap(1).wait_recv()
    turn(0)
    by_core(middle)
    turn(1)
    by_core(second_half)
    swap(2).wait_recv()
    swap(3).wait_recv()
    turn(2)
    turn(3)

    def sent(t):
        amount = codes.at[t, :, pl.ds(0, 15 * 256)]
        rows = peaks.at[t, pl.ds(0, 15)]
        return (
            remote(amount, amount, v_send.at[t], v_recv.at[t], sibling),
            remote(rows, rows, s_send.at[t], s_recv.at[t], sibling),
        )

    for t in range(TURNS):
        for copies in sent(t):
            copies.wait_recv()
        split(t)
        place(t)
        lax.fori_loop(2 * t, 2 * t + 2, smooth, 0)
    by_core(close)
    ids.wait_send()
    for t in range(TURNS):
        swap(t).wait_send()
        for copies in sent(t):
            copies.wait_send()


def unmix(owner_order, dictionary, residual, coefs, pixel_of):
    hbm = pl.BlockSpec(memory_space=pltpu.HBM)
    dma = pltpu.SemaphoreType.DMA
    return pl.pallas_call(
        unmix_kernel,
        name="unmix",
        out_shape=jax.ShapeDtypeStruct((64, 32, 128), jnp.float32),
        in_specs=[hbm] * 5,
        out_specs=pl.BlockSpec(memory_space=pltpu.VMEM),
        scratch_shapes=[
            pltpu.SMEM((32,), jnp.int32),
            pltpu.VMEM((TURNS, 16, 4096), jnp.int16),
            pltpu.VMEM((TURNS, 16, 1, 256), jnp.float32),
            pltpu.VMEM((256, 128), jnp.float32),
            pltpu.VMEM((16, 1, 256), jnp.int32),
            pltpu.VMEM((256, TURNS, 256), jnp.bfloat16),
            pltpu.VMEM((TURNS, 256, 256), jnp.float32),
            pltpu.VMEM((2, 2, 16, 4, 64, 128), jnp.bfloat16),
            pltpu.VMEM((2, 16, 16, 128), jnp.bfloat16),
            pltpu.VMEM((256, 2048), jnp.bfloat16),
            pltpu.VMEM((256, 2048), jnp.bfloat16),
            pltpu.VMEM((TURNS, 256, 256), jnp.int16),
            pltpu.VMEM((16 * GROUPS, 4096), jnp.bfloat16),
            pltpu.VMEM((4096, SPAN), jnp.bfloat16),
            pltpu.VMEM((32 * GROUPS, 4096), jnp.bfloat16),
            pltpu.VMEM((32, 64, 128), jnp.float32),
            dma,
            dma,
            dma,
            dma,
            dma,
            dma,
            dma((2, 4, TURNS)),
            dma((2, 4, TURNS)),
            dma((TURNS,)),
            dma((TURNS,)),
            dma,
            dma,
            dma((TURNS,)),
            dma((TURNS,)),
            dma((TURNS,)),
            dma((TURNS,)),
            dma((5,)),
        ],
        compiler_params=pltpu.CompilerParams(collective_id=0, has_side_effects=True, vmem_limit_bytes=60 << 20),
    )(owner_order, dictionary, residual, coefs, pixel_of)


def per_device(residual_in, coefs_in, dictionary, owner_order, pixel_of):
    maps = unmix(owner_order, dictionary, residual_in[0], coefs_in[0], pixel_of)
    return maps.reshape(1, TURNS, 16, 32, MAP_W)


def solution(mesh):
    placed = (
        P("field", "point", None),
        P("field", "point", None, None),
        P("field", None),
        P(),
        P("field", "point"),
    )
    return jax.shard_map(
        per_device,
        mesh=mesh,
        in_specs=placed,
        out_specs=P("field", None, "point", None, None),
        check_vma=False,
    )
```

```python
import functools

import jax
import jax.numpy as jnp
from jax import lax
from jax.experimental import pallas as pl
from jax.experimental.pallas import tpu as pltpu
from jax.sharding import PartitionSpec as P

TURNS = 4
SWEEPS = 4
MAP_W = 128
MESH = pl.DeviceIdType.MESH
LEVELS = 65534.0
GROUPS = 4
SPAN = 4096 // GROUPS

time_step = 0.2
edge_scale = 0.5


def dev(z, x, core, y):
    return (z // 4 * 8 + x * 2 + core, y * 4 + z % 4)


def remote(src, dst, send, recv, device):
    return pltpu.make_async_remote_copy(
        src_ref=src, dst_ref=dst, send_sem=send, recv_sem=recv, device_id=device, device_id_type=MESH
    )


def nt(a, b):
    return lax.dot_general(a, b, (((1,), (1,)), ((), ())), preferred_element_type=jnp.float32)


def unmix_kernel(
    owner_hbm,
    block,
    residual_hbm,
    coefs_hbm,
    pixel_of,
    maps,
    owner,
    codes,
    peaks,
    peak_cols,
    pixels,
    coefs_in,
    coefs,
    g,
    cand,
    residual,
    templates,
    updated,
    member,
    select,
    parts,
    state,
    a_send,
    a_recv,
    b_send,
    b_recv,
    z_send,
    z_recv,
    ring_send,
    ring_recv,
    c_send,
    c_recv,
    id_send,
    id_recv,
    v_send,
    v_recv,
    s_send,
    s_recv,
    load_sem,
):
    f = lax.axis_index("field")
    p = lax.axis_index("point")
    core = f % 2
    chip = f // 2
    x = chip % 4
    zh = f // 8
    y = p // 4
    zl = p % 4
    z = zh * 4 + zl
    a = x + core * (y - x)
    b = y + core * (x - y)
    sibling = (f + 1 - 2 * core, p)

    barrier = pltpu.get_barrier_semaphore()

    def greet(device):
        pl.semaphore_signal(barrier, inc=1, device_id=device, device_id_type=MESH)

    def greet_field(i, _):
        greet(((chip + i) % 16 * 2 + core, p))
        return _

    lax.fori_loop(1, 16, greet_field, 0)

    def greet_z(i, _):
        @pl.when(i % 4 != 0)
        def _greet():
            greet(dev((z + i) % 16, x, core, y))

        return _

    lax.fori_loop(1, 16, greet_z, 0)

    def greet_point(i, _):
        to = (p + i) % 16

        @pl.when(to // 4 != y)
        def _greet():
            greet((f, to))

        return _

    lax.fori_loop(1, 16, greet_point, 0)
    greet(sibling)
    lanes = pl.ds(pl.multiple_of(p * 128, 128), 128)

    def tile_of(to):
        tile = to // 8 * 8 + to % 4 * 2 + to // 4 % 2
        return block.at[pl.ds(pl.multiple_of(tile * 16, 16), 16), lanes]

    load_own = pltpu.make_async_copy(tile_of(chip), cand.at[core, chip], load_sem.at[0])
    load_owner = pltpu.make_async_copy(owner_hbm, owner, load_sem.at[1])
    load_pixels = pltpu.make_async_copy(pixel_of, pixels.at[p], load_sem.at[2])
    load_coefs = pltpu.make_async_copy(coefs_hbm, coefs_in, load_sem.at[3])
    load_residual = pltpu.make_async_copy(residual_hbm, residual, load_sem.at[4])
    load_own.start()
    load_owner.start()
    load_pixels.start()
    load_coefs.start()
    load_residual.start()
    pl.semaphore_wait(barrier, 15 + 12 + 12 + 1)

    def scatter(i, _):
        to = (chip + 4 * ((i // 4 + 2) % 4) + i % 4) % 16

        @pl.when(to != chip)
        def _send():
            remote(tile_of(to), cand.at[core, chip], a_send, a_recv, (to * 2 + core, p)).start()

        return _

    lax.fori_loop(0, 16, scatter, 0)

    def tell_pixels(i, _):
        remote(pixel_of, pixels.at[p], id_send, id_recv, (f, (p + i) % 16)).start()
        return _

    lax.fori_loop(1, 16, tell_pixels, 0)
    load_own.wait()
    load_owner.wait()
    all_a = remote(cand.at[0, pl.ds(0, 15)], cand.at[0, pl.ds(0, 15)], a_send, a_recv, sibling)
    all_a.wait_recv()
    both = remote(cand.at[core], cand.at[core], b_send, b_recv, sibling)
    both.start()
    both.wait()

    for tt in range(2):
        o = owner[core + 2 * tt]
        g[core, tt, zh // 2, a, b, zl, zh % 2] = cand[o % 2, o // 2]

    def along_z(i, _):
        part = g.at[core, :, zh // 2, a, b, zl, zh % 2]
        step = 8 + (i + 1) // 2 * (1 - i % 2 * 2)
        remote(part, part, z_send, z_recv, dev((z + step) % 16, x, core, y)).start()
        return _

    lax.fori_loop(0, 15, along_z, 0)
    load_coefs.wait()
    for t in range(TURNS):
        coefs[t] = coefs_in[:, t, :].astype(jnp.float32).T
    amount = templates.at[pl.ds(0, 240), pl.ds(0, 256)]
    all_z = remote(amount, amount, z_send, z_recv, sibling)
    all_z.wait_recv()

    def ring(stage, neighbour, region):
        def make(t, kind):
            offset, half, to = ((0, None, 1), (0, None, 3), (3, 0, 1), (1, 1, 3))[kind]
            ref = g.at[region(t, offset, half)]
            return remote(ref, ref, ring_send.at[stage, kind, t], ring_recv.at[stage, kind, t], neighbour(to))

        def start(t):
            make(t, 0).start()
            make(t, 1).start()

        def forward(t):
            make(t, 0).wait_recv()
            make(t, 2).start()
            make(t, 1).wait_recv()
            make(t, 3).start()

        def finish(t):
            make(t, 2).wait_recv()
            make(t, 3).wait_recv()

        def drain(t):
            for kind in range(4):
                make(t, kind).wait_send()

        return start, forward, finish, drain

    def first_neighbour(step):
        return dev(z, (x + core * step) % 4, core, (y + (1 - core) * step) % 4)

    def last_neighbour(step):
        return dev(z, (x + (1 - core) * step) % 4, core, (y + core * step) % 4)

    def mid_region(t, offset, half):
        low = pl.ds(0, 4) if half is None else pl.ds(2 * half, 2)
        return (core, t // 2, t % 2, a, (b + offset) % 4, low)

    def last_region(t, offset, half):
        firsts = pl.ds(0, 4) if half is None else pl.ds(2 * half, 2)
        return (core, t // 2, t % 2, (a + offset) % 4, firsts)

    def swap(t):
        part = g.at[core, t // 2, t % 2]
        return remote(part, part, c_send.at[t], c_recv.at[t], sibling)

    mid = ring(0, first_neighbour, mid_region)
    last = ring(1, last_neighbour, last_region)

    def share(t):
        last[2](t)
        swap(t).start()

    def send_rows(t, to):
        rows = pl.ds(pl.multiple_of(to * 16, 16), 16)
        points = pl.ds(pl.multiple_of(p * 256, 256), 256)
        return updated.at[t, rows], codes.at[t, :, points]

    def turn(t):
        for q in range(16):
            for k in range(8):
                ends = (k % 4, q // 4) if t % 2 == 0 else (q // 4, k % 4)
                tiles = g[t % 2, t // 2, k // 4, ends[0], ends[1], q % 4]
                templates[32 * k : 32 * (k + 1), 128 * q : 128 * (q + 1)] = tiles.reshape(32, 128)
        gram = nt(templates[...], templates[...])
        step = 1.0 / jnp.sum(jnp.abs(gram), axis=1, keepdims=True)
        before = coefs[t]
        after = jnp.maximum(before + step * nt(templates[...], residual[...]), 0.0)
        peak = jnp.max(after, axis=1, keepdims=True)
        share_of_peak = after / jnp.where(peak > 0.0, peak, 1.0)
        updated[t] = (jnp.floor(share_of_peak * LEVELS + 0.5) - LEVELS / 2).astype(jnp.int32).astype(jnp.int16)
        peaks[t, p] = jnp.broadcast_to(peak, (256, 128)).T[0:1]

        def deliver(i, _):
            to = (p + i) % 16
            src, dst = send_rows(t, to)
            remote(src, dst, v_send.at[t], v_recv.at[t], (f, to)).start()
            remote(peaks.at[t, p], peaks.at[t, p], s_send.at[t], s_recv.at[t], (f, to)).start()
            return _

        lax.fori_loop(1, 16, deliver, 0)
        rows = pl.ds(pl.multiple_of(p * 16, 16), 16)
        codes[t, :, pl.ds(pl.multiple_of(p * 256, 256), 256)] = updated[t, rows, :]
        if t + 1 < TURNS:
            change = (after - before).astype(jnp.bfloat16)
            for q in range(4):
                cols = slice(512 * q, 512 * (q + 1))
                moved = lax.dot_general(
                    change, templates[:, cols], (((0,), (0,)), ((), ())), preferred_element_type=jnp.float32
                )
                residual[:, cols] = (residual[:, cols].astype(jnp.float32) - moved).astype(jnp.bfloat16)

    def spread(q, _):
        points = pl.ds(pl.multiple_of(q * 256, 256), 256)
        ids = pixels[q]
        for h in range(GROUPS):
            here = jnp.where(ids // SPAN == h, 1.0, 0.0)
            member[16 * h : 16 * h + 16, points] = jnp.broadcast_to(here, (16, 256)).astype(jnp.bfloat16)
        column = jnp.broadcast_to(ids, (8, 256)).T[:, 0:1] % SPAN
        lane = lax.broadcasted_iota(jnp.int32, (256, SPAN), 1)
        select[points, :] = jnp.where(column == lane, 1.0, 0.0).astype(jnp.bfloat16)
        return _

    def split(t):
        peak_cols[:, 0:16] = peaks[t].reshape(16, 256).T
        own_peaks = peak_cols[pl.ds(pl.multiple_of(p * 16, 16), 16), :] * (1.0 / LEVELS)
        source = lax.broadcasted_iota(jnp.int32, (16, 128), 1)

        def one(q, _):
            points = pl.ds(pl.multiple_of(q * 256, 256), 256)
            scale = jnp.sum(jnp.where(source == q, own_peaks, 0.0), axis=1, keepdims=True)
            v = (codes[t, :, points].astype(jnp.int32).astype(jnp.float32) + LEVELS / 2) * scale
            high = v.astype(jnp.bfloat16)
            rest = (v - high.astype(jnp.float32)).astype(jnp.bfloat16)
            for h in range(GROUPS):
                here = member[16 * h : 16 * h + 16, points]
                row = 64 * h + t % 2 * 16
                parts[row : row + 16, points] = high * here
                parts[row + 32 : row + 48, points] = rest * here
            return _

        lax.fori_loop(0, 16, one, 0, unroll=4)

    def place(pair):
        for n in range(SPAN // 256):
            placed = jnp.dot(
                parts[...], select[:, 256 * n : 256 * (n + 1)], preferred_element_type=jnp.float32
            )
            for h in range(GROUPS):
                whole = placed[64 * h : 64 * h + 32] + placed[64 * h + 32 : 64 * h + 64]
                for r in range(2):
                    row = h * (SPAN // 128) + 2 * n + r
                    state[row, 32 * pair : 32 * pair + 32] = whole[:, 128 * r : 128 * (r + 1)]

    def flow(d):
        scaled = d * (1.0 / edge_scale)
        return d / (1.0 + scaled * scaled)

    def smooth(group, _):
        last = lax.broadcasted_iota(jnp.int32, (32, 8, 128), 2) == 127
        rows = pl.ds(pl.multiple_of(group * 8, 8), 8)
        u = state[:, rows, :]
        for repeat in range(SWEEPS):
            right = jnp.where(last, 0.0, flow(pltpu.roll(u, 127, 2) - u))
            down = flow(u[1:] - u[:-1])
            none = jnp.zeros((1, 8, 128), jnp.float32)
            total = (right - pltpu.roll(right, 1, 2)) + (
                jnp.concatenate([down, none], axis=0) - jnp.concatenate([none, down], axis=0)
            )
            u = u + time_step * total
        for i in range(32):
            maps[rows, i, :] = u[i]
        return _

    for t in range(TURNS):
        mid[0](t)
    ids = remote(pixels.at[pl.ds(0, 15)], pixels.at[pl.ds(0, 15)], id_send, id_recv, sibling)
    load_pixels.wait()
    ids.wait_recv()
    lax.fori_loop(0, 4, spread, 0)
    for t in range(TURNS):
        mid[1](t)
    lax.fori_loop(4, 8, spread, 0)
    for t in range(TURNS):
        mid[2](t)
        if t < 2:
            last[0](t)
    lax.fori_loop(8, 16, spread, 0)
    load_residual.wait()
    last[1](0)
    last[0](2)
    last[1](1)
    last[0](3)
    share(0)
    last[1](2)
    share(1)
    swap(0).wait_recv()
    swap(1).wait_recv()
    turn(0)
    last[1](3)
    share(2)
    turn(1)
    share(3)
    swap(2).wait_recv()
    swap(3).wait_recv()
    turn(2)
    turn(3)

    def sent(t):
        amount = codes.at[t, :, pl.ds(0, 15 * 256)]
        rows = peaks.at[t, pl.ds(0, 15)]
        return (
            remote(amount, amount, v_send.at[t], v_recv.at[t], sibling),
            remote(rows, rows, s_send.at[t], s_recv.at[t], sibling),
        )

    for pair in range(2):
        for t in (2 * pair, 2 * pair + 1):
            for copies in sent(t):
                copies.wait_recv()
            split(t)
        place(pair)
        lax.fori_loop(4 * pair, 4 * pair + 4, smooth, 0)
    all_a.wait_send()
    all_z.wait_send()
    ids.wait_send()
    for t in range(TURNS):
        mid[3](t)
        last[3](t)
        swap(t).wait_send()
        for copies in sent(t):
            copies.wait_send()


def unmix(owner_order, dictionary, residual, coefs, pixel_of):
    hbm = pl.BlockSpec(memory_space=pltpu.HBM)
    dma = pltpu.SemaphoreType.DMA
    return pl.pallas_call(
        unmix_kernel,
        name="unmix",
        out_shape=jax.ShapeDtypeStruct((64, 32, 128), jnp.float32),
        in_specs=[hbm] * 5,
        out_specs=pl.BlockSpec(memory_space=pltpu.VMEM),
        scratch_shapes=[
            pltpu.SMEM((32,), jnp.int32),
            pltpu.VMEM((TURNS, 16, 4096), jnp.int16),
            pltpu.VMEM((TURNS, 16, 1, 256), jnp.float32),
            pltpu.VMEM((256, 128), jnp.float32),
            pltpu.VMEM((16, 1, 256), jnp.int32),
            pltpu.VMEM((256, TURNS, 256), jnp.bfloat16),
            pltpu.VMEM((TURNS, 256, 256), jnp.float32),
            pltpu.VMEM((2, 2, 2, 4, 4, 4, 2, 16, 128), jnp.bfloat16),
            pltpu.VMEM((2, 16, 16, 128), jnp.bfloat16),
            pltpu.VMEM((256, 2048), jnp.bfloat16),
            pltpu.VMEM((256, 2048), jnp.bfloat16),
            pltpu.VMEM((TURNS, 256, 256), jnp.int16),
            pltpu.VMEM((16 * GROUPS, 4096), jnp.bfloat16),
            pltpu.VMEM((4096, SPAN), jnp.bfloat16),
            pltpu.VMEM((64 * GROUPS, 4096), jnp.bfloat16),
            pltpu.VMEM((32, 64, 128), jnp.float32),
            dma,
            dma,
            dma,
            dma,
            dma,
            dma,
            dma((2, 4, TURNS)),
            dma((2, 4, TURNS)),
            dma((TURNS,)),
            dma((TURNS,)),
            dma,
            dma,
            dma((TURNS,)),
            dma((TURNS,)),
            dma((TURNS,)),
            dma((TURNS,)),
            dma((5,)),
        ],
        compiler_params=pltpu.CompilerParams(collective_id=0, has_side_effects=True, vmem_limit_bytes=60 << 20),
    )(owner_order, dictionary, residual, coefs, pixel_of)


def per_device(residual_in, coefs_in, dictionary, owner_order, pixel_of):
    maps = unmix(owner_order, dictionary, residual_in[0], coefs_in[0], pixel_of)
    return maps.reshape(1, TURNS, 16, 32, MAP_W)


def solution(mesh):
    placed = (
        P("field", "point", None),
        P("field", "point", None, None),
        P("field", None),
        P(),
        P("field", "point"),
    )
    return jax.shard_map(
        per_device,
        mesh=mesh,
        in_specs=placed,
        out_specs=P("field", None, "point", None, None),
        check_vma=False,
    )
```

```python
import functools

import jax
import jax.numpy as jnp
from jax import lax
from jax.experimental import pallas as pl
from jax.experimental.pallas import tpu as pltpu
from jax.sharding import PartitionSpec as P

TURNS = 4
SWEEPS = 4
MAP_W = 128
MESH = pl.DeviceIdType.MESH
LEVELS = 65534.0
GROUPS = 4
SPAN = 4096 // GROUPS

time_step = 0.2
edge_scale = 0.5


def dev(z, x, core, y):
    return (z // 4 * 8 + x * 2 + core, y * 4 + z % 4)


def remote(src, dst, send, recv, device):
    return pltpu.make_async_remote_copy(
        src_ref=src, dst_ref=dst, send_sem=send, recv_sem=recv, device_id=device, device_id_type=MESH
    )


def nt(a, b):
    return lax.dot_general(a, b, (((1,), (1,)), ((), ())), preferred_element_type=jnp.float32)


def flow(d):
    scaled = d * (1.0 / edge_scale)
    return d / (1.0 + scaled * scaled)


def smooth(state, maps, group):
    edge = lax.broadcasted_iota(jnp.int32, (32, 8, 128), 2) == 127
    rows = pl.ds(pl.multiple_of(group * 8, 8), 8)
    u = state[:, rows, :]
    for repeat in range(SWEEPS):
        right = jnp.where(edge, 0.0, flow(pltpu.roll(u, 127, 2) - u))
        down = flow(u[1:] - u[:-1])
        none = jnp.zeros((1, 8, 128), jnp.float32)
        total = (right - pltpu.roll(right, 1, 2)) + (
            jnp.concatenate([down, none], axis=0) - jnp.concatenate([none, down], axis=0)
        )
        u = u + time_step * total
    for i in range(32):
        maps[rows, i, :] = u[i]


def unmix_kernel(
    owner_hbm,
    block,
    residual_hbm,
    coefs_hbm,
    pixel_of,
    maps_hbm,
    late_hbm,
    owner,
    codes,
    peaks,
    peak_cols,
    pixels,
    coefs_in,
    coefs,
    g,
    cand,
    residual,
    templates,
    updated,
    member,
    select,
    parts,
    early,
    late,
    maps,
    a_send,
    a_recv,
    b_send,
    b_recv,
    z_send,
    z_recv,
    ring_send,
    ring_recv,
    c_send,
    c_recv,
    id_send,
    id_recv,
    v_send,
    v_recv,
    s_send,
    s_recv,
    load_sem,
):
    f = lax.axis_index("field")
    p = lax.axis_index("point")
    core = f % 2
    chip = f // 2
    x = chip % 4
    zh = f // 8
    y = p // 4
    zl = p % 4
    z = zh * 4 + zl
    a = x + core * (y - x)
    b = y + core * (x - y)
    sibling = (f + 1 - 2 * core, p)

    barrier = pltpu.get_barrier_semaphore()

    def greet(device):
        pl.semaphore_signal(barrier, inc=1, device_id=device, device_id_type=MESH)

    def greet_field(i, _):
        greet(((chip + i) % 16 * 2 + core, p))
        return _

    lax.fori_loop(1, 16, greet_field, 0)

    def greet_z(i, _):
        @pl.when(i % 4 != 0)
        def _greet():
            greet(dev((z + i) % 16, x, core, y))

        return _

    lax.fori_loop(1, 16, greet_z, 0)

    def greet_point(i, _):
        to = (p + i) % 16

        @pl.when(to // 4 != y)
        def _greet():
            greet((f, to))

        return _

    lax.fori_loop(1, 16, greet_point, 0)
    greet(sibling)
    lanes = pl.ds(pl.multiple_of(p * 128, 128), 128)

    def tile_of(to):
        tile = to // 8 * 8 + to % 4 * 2 + to // 4 % 2
        return block.at[pl.ds(pl.multiple_of(tile * 16, 16), 16), lanes]

    load_own = pltpu.make_async_copy(tile_of(chip), cand.at[core, chip], load_sem.at[0])
    load_owner = pltpu.make_async_copy(owner_hbm, owner, load_sem.at[1])
    load_pixels = pltpu.make_async_copy(pixel_of, pixels.at[p], load_sem.at[2])
    load_coefs = pltpu.make_async_copy(coefs_hbm, coefs_in, load_sem.at[3])
    load_residual = pltpu.make_async_copy(residual_hbm, residual, load_sem.at[4])
    load_own.start()
    load_owner.start()
    load_pixels.start()
    load_coefs.start()
    load_residual.start()
    pl.semaphore_wait(barrier, 15 + 12 + 12 + 1)

    def scatter(i, _):
        to = (chip + 4 * ((i // 4 + 2) % 4) + i % 4) % 16

        @pl.when(to != chip)
        def _send():
            remote(tile_of(to), cand.at[core, chip], a_send, a_recv, (to * 2 + core, p)).start()

        return _

    lax.fori_loop(0, 16, scatter, 0)

    def tell_pixels(i, _):
        remote(pixel_of, pixels.at[p], id_send, id_recv, (f, (p + i) % 16)).start()
        return _

    lax.fori_loop(1, 16, tell_pixels, 0)
    load_own.wait()
    load_owner.wait()
    all_a = remote(cand.at[0, pl.ds(0, 15)], cand.at[0, pl.ds(0, 15)], a_send, a_recv, sibling)
    all_a.wait_recv()
    both = remote(cand.at[core], cand.at[core], b_send, b_recv, sibling)
    both.start()
    both.wait()

    for tt in range(2):
        o = owner[core + 2 * tt]
        g[core, tt, zh // 2, a, b, zl, zh % 2] = cand[o % 2, o // 2]

    def along_z(i, _):
        part = g.at[core, :, zh // 2, a, b, zl, zh % 2]
        step = 8 + (i + 1) // 2 * (1 - i % 2 * 2)
        remote(part, part, z_send, z_recv, dev((z + step) % 16, x, core, y)).start()
        return _

    lax.fori_loop(0, 15, along_z, 0)
    load_coefs.wait()
    for t in range(TURNS):
        coefs[t] = coefs_in[:, t, :].astype(jnp.float32).T
    amount = templates.at[pl.ds(0, 240), pl.ds(0, 256)]
    all_z = remote(amount, amount, z_send, z_recv, sibling)
    all_z.wait_recv()

    def ring(stage, neighbour, region):
        def make(t, kind):
            offset, half, to = ((0, None, 1), (0, None, 3), (3, 0, 1), (1, 1, 3))[kind]
            ref = g.at[region(t, offset, half)]
            return remote(ref, ref, ring_send.at[stage, kind, t], ring_recv.at[stage, kind, t], neighbour(to))

        def start(t):
            make(t, 0).start()
            make(t, 1).start()

        def forward(t):
            make(t, 0).wait_recv()
            make(t, 2).start()
            make(t, 1).wait_recv()
            make(t, 3).start()

        def finish(t):
            make(t, 2).wait_recv()
            make(t, 3).wait_recv()

        def drain(t):
            for kind in range(4):
                make(t, kind).wait_send()

        return start, forward, finish, drain

    def first_neighbour(step):
        return dev(z, (x + core * step) % 4, core, (y + (1 - core) * step) % 4)

    def last_neighbour(step):
        return dev(z, (x + (1 - core) * step) % 4, core, (y + core * step) % 4)

    def mid_region(t, offset, half):
        low = pl.ds(0, 4) if half is None else pl.ds(2 * half, 2)
        return (core, t // 2, t % 2, a, (b + offset) % 4, low)

    def last_region(t, offset, half):
        firsts = pl.ds(0, 4) if half is None else pl.ds(2 * half, 2)
        return (core, t // 2, t % 2, (a + offset) % 4, firsts)

    def swap(t):
        part = g.at[core, t // 2, t % 2]
        return remote(part, part, c_send.at[t], c_recv.at[t], sibling)

    mid = ring(0, first_neighbour, mid_region)
    last = ring(1, last_neighbour, last_region)

    def share(t):
        last[2](t)
        swap(t).start()

    def send_rows(t, to):
        rows = pl.ds(pl.multiple_of(to * 16, 16), 16)
        points = pl.ds(pl.multiple_of(p * 256, 256), 256)
        return updated.at[t, rows], codes.at[t, :, points]

    def turn(t):
        for q in range(16):
            for k in range(8):
                ends = (k % 4, q // 4) if t % 2 == 0 else (q // 4, k % 4)
                tiles = g[t % 2, t // 2, k // 4, ends[0], ends[1], q % 4]
                templates[32 * k : 32 * (k + 1), 128 * q : 128 * (q + 1)] = tiles.reshape(32, 128)
        gram = nt(templates[...], templates[...])
        step = 1.0 / jnp.sum(jnp.abs(gram), axis=1, keepdims=True)
        before = coefs[t]
        after = jnp.maximum(before + step * nt(templates[...], residual[...]), 0.0)
        peak = jnp.max(after, axis=1, keepdims=True)
        share_of_peak = after / jnp.where(peak > 0.0, peak, 1.0)
        updated[t] = (jnp.floor(share_of_peak * LEVELS + 0.5) - LEVELS / 2).astype(jnp.int32).astype(jnp.int16)
        peaks[t // 2, p, :, 256 * (t % 2) : 256 * (t % 2) + 256] = jnp.broadcast_to(peak, (256, 128)).T[0:1]

        def deliver(i, _):
            to = (p + i) % 16
            src, dst = send_rows(t, to)
            remote(src, dst, v_send.at[t], v_recv.at[t], (f, to)).start()
            if t % 2 == 1:
                pair = peaks.at[t // 2, p]
                remote(pair, pair, s_send.at[t // 2], s_recv.at[t // 2], (f, to)).start()
            return _

        lax.fori_loop(1, 16, deliver, 0)
        rows = pl.ds(pl.multiple_of(p * 16, 16), 16)
        codes[t, :, pl.ds(pl.multiple_of(p * 256, 256), 256)] = updated[t, rows, :]
        if t + 1 < TURNS:
            change = (after - before).astype(jnp.bfloat16)
            for q in range(4):
                cols = slice(512 * q, 512 * (q + 1))
                moved = lax.dot_general(
                    change, templates[:, cols], (((0,), (0,)), ((), ())), preferred_element_type=jnp.float32
                )
                residual[:, cols] = (residual[:, cols].astype(jnp.float32) - moved).astype(jnp.bfloat16)

    def spread(q, _):
        points = pl.ds(pl.multiple_of(q * 256, 256), 256)
        ids = pixels[q]
        for h in range(GROUPS):
            here = jnp.where(ids // SPAN == h, 1.0, 0.0)
            member[16 * h : 16 * h + 16, points] = jnp.broadcast_to(here, (16, 256)).astype(jnp.bfloat16)
        column = jnp.broadcast_to(ids, (8, 256)).T[:, 0:1] % SPAN
        lane = lax.broadcasted_iota(jnp.int32, (256, SPAN), 1)
        select[points, :] = jnp.where(column == lane, 1.0, 0.0).astype(jnp.bfloat16)
        return _

    def split(t):
        peak_cols[:, 0:16] = peaks[t // 2, :, :, 256 * (t % 2) : 256 * (t % 2) + 256].reshape(16, 256).T
        own_peaks = peak_cols[pl.ds(pl.multiple_of(p * 16, 16), 16), :] * (1.0 / LEVELS)
        source = lax.broadcasted_iota(jnp.int32, (16, 128), 1)

        def one(q, _):
            points = pl.ds(pl.multiple_of(q * 256, 256), 256)
            scale = jnp.sum(jnp.where(source == q, own_peaks, 0.0), axis=1, keepdims=True)
            v = (codes[t, :, points].astype(jnp.int32).astype(jnp.float32) + LEVELS / 2) * scale
            high = v.astype(jnp.bfloat16)
            rest = (v - high.astype(jnp.float32)).astype(jnp.bfloat16)
            for h in range(GROUPS):
                here = member[16 * h : 16 * h + 16, points]
                row = 64 * h + t % 2 * 16
                parts[row : row + 16, points] = high * here
                parts[row + 32 : row + 48, points] = rest * here
            return _

        lax.fori_loop(0, 16, one, 0, unroll=4)

    def place(pair):
        for n in range(SPAN // 256):
            placed = jnp.dot(
                parts[...], select[:, 256 * n : 256 * (n + 1)], preferred_element_type=jnp.float32
            )
            for h in range(GROUPS):
                whole = placed[64 * h : 64 * h + 32] + placed[64 * h + 32 : 64 * h + 64]
                for r in range(2):
                    row = h * (SPAN // 128) + 2 * n + r
                    (early, late)[pair][row] = whole[:, 128 * r : 128 * (r + 1)]

    for t in range(TURNS):
        mid[0](t)
    ids = remote(pixels.at[pl.ds(0, 15)], pixels.at[pl.ds(0, 15)], id_send, id_recv, sibling)
    load_pixels.wait()
    ids.wait_recv()
    lax.fori_loop(0, 4, spread, 0)
    for t in range(TURNS):
        mid[1](t)
    lax.fori_loop(4, 8, spread, 0)
    for t in range(TURNS):
        mid[2](t)
        if t < 2:
            last[0](t)
    lax.fori_loop(8, 16, spread, 0)
    load_residual.wait()
    last[1](0)
    last[0](2)
    last[1](1)
    last[0](3)
    share(0)
    last[1](2)
    share(1)
    swap(0).wait_recv()
    swap(1).wait_recv()
    turn(0)
    last[1](3)
    share(2)
    turn(1)
    share(3)
    swap(2).wait_recv()
    swap(3).wait_recv()
    turn(2)
    turn(3)

    def sent(t):
        amount = codes.at[t, :, pl.ds(0, 15 * 256)]
        return remote(amount, amount, v_send.at[t], v_recv.at[t], sibling)

    def sent_peaks(pair):
        rows = peaks.at[pair, pl.ds(0, 15)]
        return remote(rows, rows, s_send.at[pair], s_recv.at[pair], sibling)

    store_maps = pltpu.make_async_copy(maps, maps_hbm, load_sem.at[5])
    store_late = pltpu.make_async_copy(late, late_hbm, load_sem.at[6])
    for pair in range(2):
        sent_peaks(pair).wait_recv()
        for t in (2 * pair, 2 * pair + 1):
            sent(t).wait_recv()
            split(t)
        place(pair)
        if pair == 0:

            def smooth_early(group, _):
                smooth(early, maps, group)
                return _

            lax.fori_loop(0, 4, smooth_early, 0)
            store_maps.start()
        else:
            store_late.start()
    all_a.wait_send()
    all_z.wait_send()
    ids.wait_send()
    for t in range(TURNS):
        mid[3](t)
        last[3](t)
        swap(t).wait_send()
        sent(t).wait_send()
    for pair in range(2):
        sent_peaks(pair).wait_send()
    store_maps.wait()
    store_late.wait()


def unmix(owner_order, dictionary, residual, coefs, pixel_of):
    hbm = pl.BlockSpec(memory_space=pltpu.HBM)
    dma = pltpu.SemaphoreType.DMA
    return pl.pallas_call(
        unmix_kernel,
        name="unmix",
        out_shape=(jax.ShapeDtypeStruct((32, 32, 128), jnp.float32),) * 2,
        in_specs=[hbm] * 5,
        out_specs=(hbm,) * 2,
        scratch_shapes=[
            pltpu.SMEM((32,), jnp.int32),
            pltpu.VMEM((TURNS, 16, 4096), jnp.int16),
            pltpu.VMEM((2, 16, 1, 512), jnp.float32),
            pltpu.VMEM((256, 128), jnp.float32),
            pltpu.VMEM((16, 1, 256), jnp.int32),
            pltpu.VMEM((256, TURNS, 256), jnp.bfloat16),
            pltpu.VMEM((TURNS, 256, 256), jnp.float32),
            pltpu.VMEM((2, 2, 2, 4, 4, 4, 2, 16, 128), jnp.bfloat16),
            pltpu.VMEM((2, 16, 16, 128), jnp.bfloat16),
            pltpu.VMEM((256, 2048), jnp.bfloat16),
            pltpu.VMEM((256, 2048), jnp.bfloat16),
            pltpu.VMEM((TURNS, 256, 256), jnp.int16),
            pltpu.VMEM((16 * GROUPS, 4096), jnp.bfloat16),
            pltpu.VMEM((4096, SPAN), jnp.bfloat16),
            pltpu.VMEM((64 * GROUPS, 4096), jnp.bfloat16),
            pltpu.VMEM((32, 32, 128), jnp.float32),
            pltpu.VMEM((32, 32, 128), jnp.float32),
            pltpu.VMEM((32, 32, 128), jnp.float32),
            dma,
            dma,
            dma,
            dma,
            dma,
            dma,
            dma((2, 4, TURNS)),
            dma((2, 4, TURNS)),
            dma((TURNS,)),
            dma((TURNS,)),
            dma,
            dma,
            dma((TURNS,)),
            dma((TURNS,)),
            dma((TURNS,)),
            dma((TURNS,)),
            dma((7,)),
        ],
        compiler_params=pltpu.CompilerParams(collective_id=0, has_side_effects=True, vmem_limit_bytes=60 << 20),
    )(owner_order, dictionary, residual, coefs, pixel_of)


def finish_kernel(maps, late_hbm, out, late, smoothed, in_sems, out_sems):
    reads = []
    for group in range(4):
        rows = pl.ds(8 * group, 8)
        reads.append(pltpu.make_async_copy(late_hbm.at[:, rows], late.at[:, rows], in_sems.at[group]))
        reads[group].start()
    first = pltpu.make_async_copy(maps, out.at[pl.ds(0, 32)], out_sems.at[4])
    first.start()
    writes = []
    for group in range(4):
        reads[group].wait()
        smooth(late, smoothed, group)
        rows = pl.ds(8 * group, 8)
        writes.append(pltpu.make_async_copy(smoothed.at[rows], out.at[pl.ds(32 + 8 * group, 8)], out_sems.at[group]))
        writes[group].start()
    for write in writes:
        write.wait()
    first.wait()


def finish(maps, late):
    hbm = pl.BlockSpec(memory_space=pltpu.HBM)
    dma = pltpu.SemaphoreType.DMA
    return pl.pallas_call(
        finish_kernel,
        name="finish",
        out_shape=jax.ShapeDtypeStruct((64, 32, 128), jnp.float32),
        in_specs=[hbm, hbm],
        out_specs=hbm,
        scratch_shapes=[pltpu.VMEM((32, 32, 128), jnp.float32)] * 2 + [dma((4,)), dma((5,))],
        compiler_params=pltpu.CompilerParams(vmem_limit_bytes=60 << 20),
    )(maps, late)


def per_device(residual_in, coefs_in, dictionary, owner_order, pixel_of):
    maps = finish(*unmix(owner_order, dictionary, residual_in[0], coefs_in[0], pixel_of))
    return maps.reshape(1, TURNS, 16, 32, MAP_W)


def solution(mesh):
    placed = (
        P("field", "point", None),
        P("field", "point", None, None),
        P("field", None),
        P(),
        P("field", "point"),
    )
    return jax.shard_map(
        per_device,
        mesh=mesh,
        in_specs=placed,
        out_specs=P("field", None, "point", None, None),
        check_vma=False,
    )
```

```python
import functools

import jax
import jax.numpy as jnp
from jax import lax
from jax.experimental import pallas as pl
from jax.experimental.pallas import tpu as pltpu
from jax.sharding import PartitionSpec as P

TURNS = 4
SWEEPS = 4
MAP_W = 128
MESH = pl.DeviceIdType.MESH
LEVELS = 65534.0
GROUPS = 4
SPAN = 4096 // GROUPS

time_step = 0.2
edge_scale = 0.5


def dev(z, x, core, y):
    return (z // 4 * 8 + x * 2 + core, y * 4 + z % 4)


def remote(src, dst, send, recv, device):
    return pltpu.make_async_remote_copy(
        src_ref=src, dst_ref=dst, send_sem=send, recv_sem=recv, device_id=device, device_id_type=MESH
    )


def nt(a, b):
    return lax.dot_general(a, b, (((1,), (1,)), ((), ())), preferred_element_type=jnp.float32)


def flow(d):
    scaled = d * (1.0 / edge_scale)
    return d / (1.0 + scaled * scaled)


def smooth(state, maps, group):
    edge = lax.broadcasted_iota(jnp.int32, (32, 8, 128), 2) == 127
    rows = pl.ds(pl.multiple_of(group * 8, 8), 8)
    u = state[group]
    for repeat in range(SWEEPS):
        right = jnp.where(edge, 0.0, flow(pltpu.roll(u, 127, 2) - u))
        down = flow(u[1:] - u[:-1])
        none = jnp.zeros((1, 8, 128), jnp.float32)
        total = (right - pltpu.roll(right, 1, 2)) + (
            jnp.concatenate([down, none], axis=0) - jnp.concatenate([none, down], axis=0)
        )
        u = u + time_step * total
    for i in range(32):
        maps[rows, i, :] = u[i]


def unmix_kernel(
    owner_hbm,
    block,
    residual_hbm,
    coefs_hbm,
    pixel_of,
    maps_hbm,
    late_hbm,
    owner,
    codes,
    peaks,
    peak_cols,
    pixels,
    coefs_in,
    coefs,
    g,
    cand,
    residual,
    templates,
    updated,
    member,
    select,
    parts,
    early,
    late,
    maps,
    a_send,
    a_recv,
    b_send,
    b_recv,
    z_send,
    z_recv,
    ring_send,
    ring_recv,
    c_send,
    c_recv,
    id_send,
    id_recv,
    v_send,
    v_recv,
    s_send,
    s_recv,
    load_sem,
):
    f = lax.axis_index("field")
    p = lax.axis_index("point")
    core = f % 2
    chip = f // 2
    x = chip % 4
    zh = f // 8
    y = p // 4
    zl = p % 4
    z = zh * 4 + zl
    a = x + core * (y - x)
    b = y + core * (x - y)
    sibling = (f + 1 - 2 * core, p)

    barrier = pltpu.get_barrier_semaphore()

    def greet(device):
        pl.semaphore_signal(barrier, inc=1, device_id=device, device_id_type=MESH)

    def greet_field(i, _):
        greet(((chip + i) % 16 * 2 + core, p))
        return _

    lax.fori_loop(1, 16, greet_field, 0)

    def greet_z(i, _):
        @pl.when(i % 4 != 0)
        def _greet():
            greet(dev((z + i) % 16, x, core, y))

        return _

    lax.fori_loop(1, 16, greet_z, 0)

    def greet_point(i, _):
        to = (p + i) % 16

        @pl.when(to // 4 != y)
        def _greet():
            greet((f, to))

        return _

    lax.fori_loop(1, 16, greet_point, 0)
    greet(sibling)
    lanes = pl.ds(pl.multiple_of(p * 128, 128), 128)

    def tile_of(to):
        tile = to // 8 * 8 + to % 4 * 2 + to // 4 % 2
        return block.at[pl.ds(pl.multiple_of(tile * 16, 16), 16), lanes]

    load_own = pltpu.make_async_copy(tile_of(chip), cand.at[core, chip], load_sem.at[0])
    load_owner = pltpu.make_async_copy(owner_hbm, owner, load_sem.at[1])
    load_pixels = pltpu.make_async_copy(pixel_of, pixels.at[p], load_sem.at[2])
    load_coefs = pltpu.make_async_copy(coefs_hbm, coefs_in, load_sem.at[3])
    load_residual = pltpu.make_async_copy(residual_hbm, residual, load_sem.at[4])
    load_own.start()
    load_owner.start()
    load_pixels.start()
    load_coefs.start()
    load_residual.start()
    pl.semaphore_wait(barrier, 15 + 12 + 12 + 1)

    def scatter(i, _):
        to = (chip + 4 * ((i // 4 + 2) % 4) + i % 4) % 16

        @pl.when(to != chip)
        def _send():
            remote(tile_of(to), cand.at[core, chip], a_send, a_recv, (to * 2 + core, p)).start()

        return _

    lax.fori_loop(0, 16, scatter, 0)

    def tell_pixels(i, _):
        remote(pixel_of, pixels.at[p], id_send, id_recv, (f, (p + i) % 16)).start()
        return _

    lax.fori_loop(1, 16, tell_pixels, 0)
    load_own.wait()
    load_owner.wait()
    all_a = remote(cand.at[0, pl.ds(0, 15)], cand.at[0, pl.ds(0, 15)], a_send, a_recv, sibling)
    all_a.wait_recv()
    both = remote(cand.at[core], cand.at[core], b_send, b_recv, sibling)
    both.start()
    both.wait()

    for tt in range(2):
        o = owner[core + 2 * tt]
        g[core, tt, zh // 2, a, b, zl, zh % 2] = cand[o % 2, o // 2]

    def along_z(tt):
        def one(i, _):
            part = g.at[core, tt, zh // 2, a, b, zl, zh % 2]
            step = 8 + (i + 1) // 2 * (1 - i % 2 * 2)
            remote(part, part, z_send.at[tt], z_recv.at[tt], dev((z + step) % 16, x, core, y)).start()
            return _

        lax.fori_loop(0, 15, one, 0)

    def all_z(tt):
        amount = templates.at[pl.ds(0, 240), pl.ds(0, 128)]
        return remote(amount, amount, z_send.at[tt], z_recv.at[tt], sibling)

    along_z(0)
    along_z(1)
    load_coefs.wait()
    for t in range(TURNS):
        coefs[t] = coefs_in[:, t, :].astype(jnp.float32).T

    def ring(stage, neighbour, region):
        def make(t, kind):
            offset, half, to = ((0, None, 1), (0, None, 3), (3, 0, 1), (1, 1, 3))[kind]
            ref = g.at[region(t, offset, half)]
            return remote(ref, ref, ring_send.at[stage, kind, t], ring_recv.at[stage, kind, t], neighbour(to))

        def start(t):
            make(t, 0).start()
            make(t, 1).start()

        def forward(t):
            make(t, 0).wait_recv()
            make(t, 2).start()
            make(t, 1).wait_recv()
            make(t, 3).start()

        def finish(t):
            make(t, 2).wait_recv()
            make(t, 3).wait_recv()

        def drain(t):
            for kind in range(4):
                make(t, kind).wait_send()

        return start, forward, finish, drain

    def first_neighbour(step):
        return dev(z, (x + core * step) % 4, core, (y + (1 - core) * step) % 4)

    def last_neighbour(step):
        return dev(z, (x + (1 - core) * step) % 4, core, (y + core * step) % 4)

    def mid_region(t, offset, half):
        low = pl.ds(0, 4) if half is None else pl.ds(2 * half, 2)
        return (core, t // 2, t % 2, a, (b + offset) % 4, low)

    def last_region(t, offset, half):
        firsts = pl.ds(0, 4) if half is None else pl.ds(2 * half, 2)
        return (core, t // 2, t % 2, (a + offset) % 4, firsts)

    def swap(t):
        part = g.at[core, t // 2, t % 2]
        return remote(part, part, c_send.at[t], c_recv.at[t], sibling)

    mid = ring(0, first_neighbour, mid_region)
    last = ring(1, last_neighbour, last_region)

    def share(t):
        last[2](t)
        swap(t).start()

    def send_rows(t, to):
        rows = pl.ds(pl.multiple_of(to * 16, 16), 16)
        points = pl.ds(pl.multiple_of(p * 256, 256), 256)
        return updated.at[t, rows], codes.at[t, :, points]

    def turn(t):
        for q in range(16):
            for k in range(8):
                ends = (k % 4, q // 4) if t % 2 == 0 else (q // 4, k % 4)
                tiles = g[t % 2, t // 2, k // 4, ends[0], ends[1], q % 4]
                templates[32 * k : 32 * (k + 1), 128 * q : 128 * (q + 1)] = tiles.reshape(32, 128)
        gram = nt(templates[...], templates[...])
        step = 1.0 / jnp.sum(jnp.abs(gram), axis=1, keepdims=True)
        before = coefs[t]
        after = jnp.maximum(before + step * nt(templates[...], residual[...]), 0.0)
        peak = jnp.max(after, axis=1, keepdims=True)
        share_of_peak = after / jnp.where(peak > 0.0, peak, 1.0)
        updated[t] = (jnp.floor(share_of_peak * LEVELS + 0.5) - LEVELS / 2).astype(jnp.int32).astype(jnp.int16)
        peaks[t // 2, p, :, 256 * (t % 2) : 256 * (t % 2) + 256] = jnp.broadcast_to(peak, (256, 128)).T[0:1]

        def deliver(i, _):
            to = (p + i) % 16
            src, dst = send_rows(t, to)
            remote(src, dst, v_send.at[t], v_recv.at[t], (f, to)).start()
            if t % 2 == 1:
                pair = peaks.at[t // 2, p]
                remote(pair, pair, s_send.at[t // 2], s_recv.at[t // 2], (f, to)).start()
            return _

        lax.fori_loop(1, 16, deliver, 0)
        rows = pl.ds(pl.multiple_of(p * 16, 16), 16)
        codes[t, :, pl.ds(pl.multiple_of(p * 256, 256), 256)] = updated[t, rows, :]
        if t + 1 < TURNS:
            change = (after - before).astype(jnp.bfloat16)
            for q in range(4):
                cols = slice(512 * q, 512 * (q + 1))
                moved = lax.dot_general(
                    change, templates[:, cols], (((0,), (0,)), ((), ())), preferred_element_type=jnp.float32
                )
                residual[:, cols] = (residual[:, cols].astype(jnp.float32) - moved).astype(jnp.bfloat16)

    def spread(q, _):
        points = pl.ds(pl.multiple_of(q * 256, 256), 256)
        ids = pixels[q]
        for h in range(GROUPS):
            here = jnp.where(ids // SPAN == h, 1.0, 0.0)
            member[16 * h : 16 * h + 16, points] = jnp.broadcast_to(here, (16, 256)).astype(jnp.bfloat16)
        column = jnp.broadcast_to(ids, (8, 256)).T[:, 0:1] % SPAN
        lane = lax.broadcasted_iota(jnp.int32, (256, SPAN), 1)
        select[points, :] = jnp.where(column == lane, 1.0, 0.0).astype(jnp.bfloat16)
        return _

    def split(t):
        peak_cols[:, 0:16] = peaks[t // 2, :, :, 256 * (t % 2) : 256 * (t % 2) + 256].reshape(16, 256).T
        own_peaks = peak_cols[pl.ds(pl.multiple_of(p * 16, 16), 16), :] * (1.0 / LEVELS)
        source = lax.broadcasted_iota(jnp.int32, (16, 128), 1)

        def one(q, _):
            points = pl.ds(pl.multiple_of(q * 256, 256), 256)
            scale = jnp.sum(jnp.where(source == q, own_peaks, 0.0), axis=1, keepdims=True)
            v = (codes[t, :, points].astype(jnp.int32).astype(jnp.float32) + LEVELS / 2) * scale
            high = v.astype(jnp.bfloat16)
            rest = (v - high.astype(jnp.float32)).astype(jnp.bfloat16)
            for h in range(GROUPS):
                here = member[16 * h : 16 * h + 16, points]
                row = 64 * h + t % 2 * 16
                parts[row : row + 16, points] = high * here
                parts[row + 32 : row + 48, points] = rest * here
            return _

        lax.fori_loop(0, 16, one, 0, unroll=4)

    def place(pair):
        for n in range(SPAN // 256):
            placed = jnp.dot(
                parts[...], select[:, 256 * n : 256 * (n + 1)], preferred_element_type=jnp.float32
            )
            for h in range(GROUPS):
                whole = placed[64 * h : 64 * h + 32] + placed[64 * h + 32 : 64 * h + 64]
                for r in range(2):
                    row = h * (SPAN // 128) + 2 * n + r
                    for group in range(4):
                        (early, late)[pair][group, row] = whole[8 * group : 8 * group + 8, 128 * r : 128 * (r + 1)]

    all_z(0).wait_recv()
    mid[0](0)
    mid[0](1)
    all_z(1).wait_recv()
    mid[0](2)
    mid[0](3)
    ids = remote(pixels.at[pl.ds(0, 15)], pixels.at[pl.ds(0, 15)], id_send, id_recv, sibling)
    load_pixels.wait()
    ids.wait_recv()
    lax.fori_loop(0, 3, spread, 0)
    mid[1](0)
    mid[1](1)
    lax.fori_loop(3, 5, spread, 0)
    mid[1](2)
    mid[1](3)
    lax.fori_loop(5, 7, spread, 0)
    mid[2](0)
    last[0](0)
    mid[2](1)
    last[0](1)
    lax.fori_loop(7, 16, spread, 0)
    mid[2](2)
    mid[2](3)
    load_residual.wait()
    last[1](0)
    last[0](2)
    last[1](1)
    last[0](3)
    share(0)
    last[1](2)
    share(1)
    swap(0).wait_recv()
    swap(1).wait_recv()
    turn(0)
    last[1](3)
    share(2)
    turn(1)
    share(3)
    swap(2).wait_recv()
    swap(3).wait_recv()
    turn(2)
    turn(3)

    def sent(t):
        amount = codes.at[t, :, pl.ds(0, 15 * 256)]
        return remote(amount, amount, v_send.at[t], v_recv.at[t], sibling)

    def sent_peaks(pair):
        rows = peaks.at[pair, pl.ds(0, 15)]
        return remote(rows, rows, s_send.at[pair], s_recv.at[pair], sibling)

    store_maps = pltpu.make_async_copy(maps, maps_hbm, load_sem.at[5])
    store_late = pltpu.make_async_copy(late, late_hbm, load_sem.at[6])
    for pair in range(2):
        sent_peaks(pair).wait_recv()
        for t in (2 * pair, 2 * pair + 1):
            sent(t).wait_recv()
            split(t)
        place(pair)
        if pair == 0:

            def smooth_early(group, _):
                smooth(early, maps, group)
                return _

            lax.fori_loop(0, 4, smooth_early, 0)
            store_maps.start()
        else:
            store_late.start()
    all_a.wait_send()
    all_z(0).wait_send()
    all_z(1).wait_send()
    ids.wait_send()
    for t in range(TURNS):
        mid[3](t)
        last[3](t)
        swap(t).wait_send()
        sent(t).wait_send()
    for pair in range(2):
        sent_peaks(pair).wait_send()
    store_maps.wait()
    store_late.wait()


def unmix(owner_order, dictionary, residual, coefs, pixel_of):
    hbm = pl.BlockSpec(memory_space=pltpu.HBM)
    dma = pltpu.SemaphoreType.DMA
    return pl.pallas_call(
        unmix_kernel,
        name="unmix",
        out_shape=(
            jax.ShapeDtypeStruct((32, 32, 128), jnp.float32),
            jax.ShapeDtypeStruct((4, 32, 8, 128), jnp.float32),
        ),
        in_specs=[hbm] * 5,
        out_specs=(hbm,) * 2,
        scratch_shapes=[
            pltpu.SMEM((32,), jnp.int32),
            pltpu.VMEM((TURNS, 16, 4096), jnp.int16),
            pltpu.VMEM((2, 16, 1, 512), jnp.float32),
            pltpu.VMEM((256, 128), jnp.float32),
            pltpu.VMEM((16, 1, 256), jnp.int32),
            pltpu.VMEM((256, TURNS, 256), jnp.bfloat16),
            pltpu.VMEM((TURNS, 256, 256), jnp.float32),
            pltpu.VMEM((2, 2, 2, 4, 4, 4, 2, 16, 128), jnp.bfloat16),
            pltpu.VMEM((2, 16, 16, 128), jnp.bfloat16),
            pltpu.VMEM((256, 2048), jnp.bfloat16),
            pltpu.VMEM((256, 2048), jnp.bfloat16),
            pltpu.VMEM((TURNS, 256, 256), jnp.int16),
            pltpu.VMEM((16 * GROUPS, 4096), jnp.bfloat16),
            pltpu.VMEM((4096, SPAN), jnp.bfloat16),
            pltpu.VMEM((64 * GROUPS, 4096), jnp.bfloat16),
            pltpu.VMEM((4, 32, 8, 128), jnp.float32),
            pltpu.VMEM((4, 32, 8, 128), jnp.float32),
            pltpu.VMEM((32, 32, 128), jnp.float32),
            dma,
            dma,
            dma,
            dma,
            dma((2,)),
            dma((2,)),
            dma((2, 4, TURNS)),
            dma((2, 4, TURNS)),
            dma((TURNS,)),
            dma((TURNS,)),
            dma,
            dma,
            dma((TURNS,)),
            dma((TURNS,)),
            dma((TURNS,)),
            dma((TURNS,)),
            dma((7,)),
        ],
        compiler_params=pltpu.CompilerParams(collective_id=0, has_side_effects=True, vmem_limit_bytes=60 << 20),
    )(owner_order, dictionary, residual, coefs, pixel_of)


def finish_kernel(maps_hbm, late_hbm, out, maps, late, smoothed, in_sems, out_sems):
    reads = []
    for group in range(4):
        reads.append(pltpu.make_async_copy(late_hbm.at[group], late.at[group], in_sems.at[group]))
        reads[group].start()
    read_maps = pltpu.make_async_copy(maps_hbm, maps, in_sems.at[4])
    read_maps.start()
    first = pltpu.make_async_copy(maps, out.at[pl.ds(0, 32)], out_sems.at[4])
    writes = []
    for group in range(4):
        reads[group].wait()
        smooth(late, smoothed, group)
        rows = pl.ds(8 * group, 8)
        writes.append(pltpu.make_async_copy(smoothed.at[rows], out.at[pl.ds(32 + 8 * group, 8)], out_sems.at[group]))
        writes[group].start()
        if group == 0:
            read_maps.wait()
            first.start()
    for write in writes:
        write.wait()
    first.wait()


def finish(maps, late):
    hbm = pl.BlockSpec(memory_space=pltpu.HBM)
    dma = pltpu.SemaphoreType.DMA
    return pl.pallas_call(
        finish_kernel,
        name="finish",
        out_shape=jax.ShapeDtypeStruct((64, 32, 128), jnp.float32),
        in_specs=[hbm, hbm],
        out_specs=hbm,
        scratch_shapes=[
            pltpu.VMEM((32, 32, 128), jnp.float32),
            pltpu.VMEM((4, 32, 8, 128), jnp.float32),
            pltpu.VMEM((32, 32, 128), jnp.float32),
            dma((5,)),
            dma((5,)),
        ],
        compiler_params=pltpu.CompilerParams(vmem_limit_bytes=60 << 20),
    )(maps, late)


def per_device(residual_in, coefs_in, dictionary, owner_order, pixel_of):
    maps = finish(*unmix(owner_order, dictionary, residual_in[0], coefs_in[0], pixel_of))
    return maps.reshape(1, TURNS, 16, 32, MAP_W)


def solution(mesh):
    placed = (
        P("field", "point", None),
        P("field", "point", None, None),
        P("field", None),
        P(),
        P("field", "point"),
    )
    return jax.shard_map(
        per_device,
        mesh=mesh,
        in_specs=placed,
        out_specs=P("field", None, "point", None, None),
        check_vma=False,
    )
```
